256 devices in a mesh: phi: 32 (over z, x), row: 2 (over core), theta: 4 (over y).
Axes of the slice: x: 4, y: 4, z: 8, core: 2. Of those that a mesh axis runs over, the one named last changes fastest.
Arguments:
- density: float32 [16, 32, 4096], P('theta', 'row', 'phi'), may hold values from 0.5 to 2
- energy: float32 [16, 32, 4096], P('theta', 'row', 'phi'), may hold values from 0.5 to 2.5
- velocity: float32 [3, 16, 32, 4096], P(None, 'theta', 'row', 'phi'), may hold values from -1.2 to 1.2
- shifts: int32 [32], P('row'), may hold values from 0 to 4095, as said below
- viscosity: float32 [32], P('row'), may hold values from 0.05 to 0.3
Outputs:
- density_out: float32 [16, 32, 4096], P('theta', 'row', 'phi')
- energy_out: float32 [16, 32, 4096], P('theta', 'row', 'phi')
- velocity_out: float32 [3, 16, 32, 4096], P(None, 'theta', 'row', 'phi')
The draws below stay inside these ranges and needn't reach their ends.
Inputs may be any that keep to these rules, and one draw needn't show every extreme that they name: `shifts`: in each aligned block of 16 radii at least one radius has an offset between 1984 and 2111, and at least one radius has an offset between 1 and 64.
All inputs are finite; a program needn't handle non-finite values.
Results may differ from the reference program's by a relative error of at most 0.00002.
Values sent between devices are 32-bit elements; how exact they have to be, the bound alone decides.
No kernel may reach another device: no remote copies, remote signals or barrier semaphores. Data moves between devices by JAX's collectives and lax.ppermute only.
A program may use at most 64 MiB of HBM per device.

```python
import math
import jax
import jax.numpy as jnp
from jax import lax

CPHI = 128
CR = 16
NPHI = 4096
NR = 32
NTH = 16


def draw_shifts(key, part):
    base_key = jax.random.fold_in(key, 7)
    key_base, key_near, key_pick, key_small, key_other = jax.random.split(base_key, 5)
    uniform_shift = jax.random.randint(key_base, (NR,), 0, NPHI)
    near_half = NPHI // 2 + jax.random.randint(key_near, (NR,), -(CPHI // 2), CPHI // 2)
    small_shift = 1 + jax.random.randint(key_small, (NR,), 0, CPHI // 2)
    picked = jax.random.randint(key_pick, (NR // CR,), 0, CR)
    other = (picked + 1 + jax.random.randint(key_other, (NR // CR,), 0, CR - 1)) % CR
    within = lax.iota(jnp.int32, NR) % CR
    chosen = within == jnp.repeat(picked, CR, total_repeat_length=NR)
    second = within == jnp.repeat(other, CR, total_repeat_length=NR)
    result = jnp.where(chosen, near_half, jnp.where(second, small_shift, uniform_shift))
    return result.astype(jnp.int32)


def steps_of(key, shape, cuts, smallest, top_value):
    gain = 1.0
    for position, shards_of in cuts:
        steps = jax.random.uniform(jax.random.fold_in(jax.random.fold_in(key, 6), position), (shards_of,), jnp.float32, smallest / len(cuts), top_value / len(cuts))
        gain = gain * jnp.repeat(jnp.exp(steps), shape[position] // shards_of).reshape((-1,) + (1,) * (len(shape) - 1 - position))
    return gain


def gaussian(rng, extent, scale, reach, cuts=(), dtype=jnp.bfloat16):
    values = scale * jax.random.normal(rng, extent, jnp.float32)
    if cuts:
        values = values * steps_of(rng, extent, cuts, -0.22, 0.18)
    return jnp.clip(values, -reach, reach).astype(dtype)


def setup_inputs(seed: int = 0) -> dict:
    splits = jax.random.split(jax.random.key(seed), 6)
    density = jnp.clip(jnp.exp(math.log(2.0) - 1.3862944 * jax.random.uniform(splits[0], (NTH, NR, NPHI), jnp.float32) ** steps_of(splits[0], (NTH, NR, NPHI), ((0, 4), (1, 2), (2, 32)), -0.2, 0.2)), 0.5, 2.0)
    energy = jnp.clip(jnp.exp(math.log(2.5) - 1.609438 * jax.random.uniform(splits[1], (NTH, NR, NPHI), jnp.float32) ** steps_of(splits[1], (NTH, NR, NPHI), ((0, 4), (1, 2), (2, 32)), -0.2, 0.2)), 0.5, 2.5)
    velocity = gaussian(splits[2], (3, NTH, NR, NPHI), 0.3, 1.2, ((1, 4), (2, 2), (3, 32)), jnp.float32)
    shifts = draw_shifts(jax.random.fold_in(splits[5], 71), 0)
    viscosity = jnp.clip(jnp.exp(math.log(0.3) - 1.7917595 * jax.random.uniform(splits[4], (NR,), jnp.float32) ** steps_of(splits[4], (NR,), ((0, 2),), -0.2, 0.2)), 0.05, 0.3)
    return dict(density=density, energy=energy, velocity=velocity, shifts=shifts, viscosity=viscosity)


GAMMA_LESS = 0.4
TIME_STEP = 0.4
DAMPING = 1.0
ROTATION = 0.5


def face_flux(quantity_lo, quantity_hi, speed_lo, speed_hi):
    return 0.25 * (speed_lo + speed_hi) * (quantity_lo + quantity_hi) - 0.5 * DAMPING * (quantity_hi - quantity_lo)


def segment_rates(padded, inv_rho):
    density, energy, radial_v, polar_v, azimuth_v = padded[0], padded[1], padded[2], padded[3], padded[4]

    def interior(quantity):
        return quantity[1:-1, 1:-1]

    def radial(quantity):
        fluxes = face_flux(quantity[1:-1, :-1], quantity[1:-1, 1:], radial_v[1:-1, :-1], radial_v[1:-1, 1:])
        return fluxes[:, 1:] - fluxes[:, :-1]

    def polar(quantity):
        fluxes = face_flux(quantity[:-1, 1:-1], quantity[1:, 1:-1], polar_v[:-1, 1:-1], polar_v[1:, 1:-1])
        return fluxes[1:] - fluxes[:-1]

    def laplace(quantity):
        return quantity[2:, 1:-1] + quantity[:-2, 1:-1] + quantity[1:-1, 2:] + quantity[1:-1, :-2] - 4.0 * interior(quantity)

    pressure = GAMMA_LESS * energy
    grad_radial = 0.5 * (pressure[1:-1, 2:] - pressure[1:-1, :-2])
    grad_polar = 0.5 * (pressure[2:, 1:-1] - pressure[:-2, 1:-1])
    rate_rho = -(radial(density) + polar(density))
    rate_energy = -(radial(energy) + polar(energy))
    rate_radial = -grad_radial * inv_rho + 0.5 * DAMPING * laplace(radial_v) + 2.0 * ROTATION * interior(azimuth_v)
    rate_polar = -grad_polar * inv_rho + 0.5 * DAMPING * laplace(polar_v)
    rate_azimuth = -(radial(azimuth_v) + polar(azimuth_v)) - 0.5 * ROTATION * interior(radial_v)
    return jnp.stack([rate_rho, rate_energy, rate_radial, rate_polar, rate_azimuth])


def reference(density, energy, velocity, shifts, viscosity):
    fields = jnp.concatenate([density[None], energy[None], velocity], 0)
    inv_rho = 1.0 / density

    def apply_rates(current):
        padded = jnp.pad(current, ((0, 0), (1, 1), (1, 1), (0, 0)))
        return segment_rates(padded, inv_rho)

    segment_one = fields + TIME_STEP * apply_rates(fields)
    segment_two = 0.5 * (fields + segment_one + TIME_STEP * apply_rates(segment_one))
    shifted = jax.vmap(lambda annulus, offset: jnp.roll(annulus, offset, axis=-1), in_axes=(2, 0), out_axes=2)(segment_two, shifts)
    behind = jnp.roll(shifted, 1, axis=-1)
    ahead = jnp.roll(shifted, -1, axis=-1)
    visc_coef = viscosity[None, :, None]
    velocity_out = shifted[2:] + visc_coef * (ahead[2:] - 2.0 * shifted[2:] + behind[2:])
    azimuth_slope = 0.5 * (ahead[4] - behind[4])
    energy_out = shifted[1] + visc_coef * shifted[0] * azimuth_slope * azimuth_slope
    return shifted[0], energy_out, velocity_out
```

```python
import jax
import jax.numpy as jnp
from jax import lax
from jax.experimental import pallas as pl
from jax.experimental.pallas import tpu as pltpu
from jax.sharding import PartitionSpec as P

GAMMA_LESS = 0.4
TIME_STEP = 0.4
DAMPING = 1.0
ROTATION = 0.5

FIELDS = 5
TH = 4
CR = 16
LANES = 128
TILE = 8
PHI = 32
PAIRS = TH * CR // PHI
ROWS = FIELDS * PAIRS


def face(q_lo, q_hi, u_lo, u_hi):
    return 0.25 * (u_lo + u_hi) * (q_lo + q_hi) - 0.5 * DAMPING * (q_hi - q_lo)


def up(value):
    return pltpu.roll(value, value.shape[0] - 1, 0)


def down(value):
    return pltpu.roll(value, 1, 0)


def rates(field, inv_rho, t):
    rho, en, vr, vt, vp = (field[f] for f in range(FIELDS))
    vr_hi = up(vr[t])
    out = []

    def divergence(q, q_hi):
        flux = face(q[t], q_hi, vr[t], vr_hi)
        radial = flux - down(flux)
        polar = face(q[t], q[t + 1], vt[t], vt[t + 1]) - face(q[t - 1], q[t], vt[t - 1], vt[t])
        return radial + polar

    en_hi = up(en[t])
    d_rho = -divergence(rho, up(rho[t]))
    d_en = -divergence(en, en_hi)
    d_vp = -divergence(vp, up(vp[t])) - 0.5 * ROTATION * vr[t]
    grad_r = 0.5 * GAMMA_LESS * (en_hi - down(en[t]))
    grad_t = 0.5 * GAMMA_LESS * (en[t + 1] - en[t - 1])
    lap_r = vr[t + 1] + vr[t - 1] + vr_hi + down(vr[t]) - 4.0 * vr[t]
    lap_t = vt[t + 1] + vt[t - 1] + up(vt[t]) + down(vt[t]) - 4.0 * vt[t]
    d_vr = -grad_r * inv_rho + 0.5 * DAMPING * lap_r + 2.0 * ROTATION * vp[t]
    d_vt = -grad_t * inv_rho + 0.5 * DAMPING * lap_t
    return d_rho, d_en, d_vr, d_vt, d_vp


def stencil_kernel(rho_ref, en_ref, vel_ref, lo_ref, hi_ref, side_ref, out_ref):
    row = lax.axis_index("row")
    theta = lax.axis_index("theta")
    pos = lax.broadcasted_iota(jnp.int32, (TILE, LANES), 0)
    near = jnp.where(row == 0, pos, TILE - 1 - pos) < TILE // 2

    def own(f, t):
        if t < 2:
            return lo_ref[f, t]
        if t >= TH + 2:
            return hi_ref[f, t - TH - 2]
        t -= 2
        return rho_ref[t] if f == 0 else en_ref[t] if f == 1 else vel_ref[f - 2, t]

    def wide(f, t):
        return jnp.concatenate([own(f, t), jnp.where(near, side_ref[f, t], 0.0)], 0)

    field = [[wide(f, t) for t in range(TH + 4)] for f in range(FIELDS)]
    first = [[None] * (TH + 4) for _ in range(FIELDS)]
    side_in = jnp.concatenate([jnp.ones((CR, LANES), jnp.bool_), near], 0)
    inverse = [None] * (TH + 4)
    for t in range(1, TH + 3):
        inside = side_in
        if t == 1:
            inside = side_in & (theta > 0)
        if t == TH + 2:
            inside = side_in & (theta < lax.axis_size("theta") - 1)
        inverse[t] = 1.0 / jnp.where(inside, field[0][t], 1.0)
        steps = rates(field, inverse[t], t)
        for f in range(FIELDS):
            first[f][t] = jnp.where(inside, field[f][t] + TIME_STEP * steps[f], 0.0)
    for t in range(2, TH + 2):
        steps = rates(first, inverse[t], t)
        for f in range(FIELDS):
            second = 0.5 * (field[f][t] + first[f][t] + TIME_STEP * steps[f])
            for p in range(PAIRS):
                start = (t - 2) * TILE * ROWS + f * PAIRS + p
                out_ref[pl.ds(start, TILE, stride=ROWS), :] = second[p * TILE : (p + 1) * TILE]


def rotate_kernel(shift_ref, visc_ref, in_ref, out_ref, twice_ref):
    mine = lax.axis_index("phi") % TILE
    lane = lax.broadcasted_iota(jnp.int32, (PHI, LANES), 1)
    for p in range(PAIRS):
        radius = mine + p * TILE
        shift = shift_ref[radius]
        nu = visc_ref[radius]
        hops = lax.shift_right_logical(shift, 7)
        rest = jnp.bitwise_and(shift, LANES - 1)
        wrapped = lane < rest

        def shifted(f):
            turned = pltpu.roll(in_ref[pl.ds(f * PAIRS + p, PHI, stride=ROWS), :], rest, 1)
            slot = f * PAIRS + p
            twice_ref[slot, :PHI] = turned
            twice_ref[slot, PHI:] = turned
            near = twice_ref[slot, pl.ds(PHI - hops, PHI), :]
            far = twice_ref[slot, pl.ds(PHI - 1 - hops, PHI), :]
            return jnp.where(wrapped, far, near)

        def put(f, value):
            out_ref[pl.ds(f * PAIRS + p, PHI, stride=ROWS), :] = value

        def sides(value):
            right = pltpu.roll(value, 1, 1)
            left = pltpu.roll(value, LANES - 1, 1)
            behind = jnp.where(lane == 0, pltpu.roll(right, 1, 0), right)
            ahead = jnp.where(lane == LANES - 1, pltpu.roll(left, PHI - 1, 0), left)
            return behind, ahead

        rho = shifted(0)
        put(0, rho)
        for f in range(2, FIELDS):
            value = shifted(f)
            behind, ahead = sides(value)
            put(f, value + nu * (ahead - 2.0 * value + behind))
            if f == FIELDS - 1:
                slope = 0.5 * (ahead - behind)
                put(1, shifted(1) + nu * rho * slope * slope)


def unpack_kernel(in_ref, rho_ref, en_ref, vel_ref):
    for f in range(FIELDS):
        for t in range(TH):
            for p in range(PAIRS):
                start = t * TILE * ROWS + f * PAIRS + p
                value = in_ref[pl.ds(start, TILE, stride=ROWS), :]
                span = slice(p * TILE, (p + 1) * TILE)
                if f == 0:
                    rho_ref[t, span] = value
                elif f == 1:
                    en_ref[t, span] = value
                else:
                    vel_ref[f - 2, t, span] = value


def vmem():
    return pl.BlockSpec(memory_space=pltpu.VMEM)


def smem():
    return pl.BlockSpec(memory_space=pltpu.SMEM)


def per_device(density, energy, velocity, shifts, viscosity):
    thetas = lax.axis_size("theta")
    rows = lax.axis_index("row")
    fields = jnp.concatenate([density[None], energy[None], velocity], 0)
    upward = [(i, i + 1) for i in range(thetas - 1)]
    downward = [(j, i) for i, j in upward]
    lo = lax.ppermute(fields[:, TH - 2 :], "theta", upward)
    hi = lax.ppermute(fields[:, :2], "theta", downward)
    tall = jnp.concatenate([lo, fields, hi], 1)
    edge = jnp.where(rows == 0, tall[:, :, CR - TILE :], tall[:, :, :TILE])
    side = lax.ppermute(edge, "row", [(0, 1), (1, 0)])
    flat = jax.ShapeDtypeStruct((PHI * ROWS, LANES), jnp.float32)
    second = pl.pallas_call(
        stencil_kernel,
        out_shape=flat,
        in_specs=[vmem()] * 6,
        out_specs=vmem(),
        name="stencil",
    )(density, energy, velocity, lo, hi, side)

    def exchange(value):
        value = lax.all_to_all(value.reshape(-1), "phi", 0, 0, tiled=True)
        return value.reshape(PHI * ROWS, LANES)

    turned = pl.pallas_call(
        rotate_kernel,
        out_shape=flat,
        in_specs=[smem(), smem(), vmem()],
        out_specs=vmem(),
        scratch_shapes=[pltpu.VMEM((ROWS, 2 * PHI, LANES), jnp.float32)],
        name="rotate",
    )(shifts, viscosity, exchange(second))
    block = jax.ShapeDtypeStruct(density.shape, jnp.float32)
    return pl.pallas_call(
        unpack_kernel,
        out_shape=(block, block, jax.ShapeDtypeStruct(velocity.shape, jnp.float32)),
        in_specs=[vmem()],
        out_specs=(vmem(), vmem(), vmem()),
        name="unpack",
    )(exchange(turned))


def solution(mesh):
    return jax.shard_map(
        per_device,
        mesh=mesh,
        in_specs=(
            P("theta", "row", "phi"),
            P("theta", "row", "phi"),
            P(None, "theta", "row", "phi"),
            P("row"),
            P("row"),
        ),
        out_specs=(
            P("theta", "row", "phi"),
            P("theta", "row", "phi"),
            P(None, "theta", "row", "phi"),
        ),
        check_vma=False,
    )
```

```python
import jax
import jax.numpy as jnp
from jax import lax
from jax.experimental import pallas as pl
from jax.experimental.pallas import tpu as pltpu
from jax.sharding import PartitionSpec as P

GAMMA_LESS = 0.4
TIME_STEP = 0.4
DAMPING = 1.0
ROTATION = 0.5

FIELDS = 5
TH = 4
CR = 16
LANES = 128
TILE = 8
PHI = 32
PAIRS = TH * CR // PHI
ROWS = FIELDS * PAIRS


def face(q_lo, q_hi, u_lo, u_hi):
    return 0.25 * (u_lo + u_hi) * (q_lo + q_hi) - 0.5 * DAMPING * (q_hi - q_lo)


def up(value):
    return pltpu.roll(value, value.shape[0] - 1, 0)


def down(value):
    return pltpu.roll(value, 1, 0)


def rates(field, inv_rho, t):
    rho, en, vr, vt, vp = (field[f] for f in range(FIELDS))
    vr_hi = up(vr[t])
    out = []

    def divergence(q, q_hi):
        flux = face(q[t], q_hi, vr[t], vr_hi)
        radial = flux - down(flux)
        polar = face(q[t], q[t + 1], vt[t], vt[t + 1]) - face(q[t - 1], q[t], vt[t - 1], vt[t])
        return radial + polar

    en_hi = up(en[t])
    d_rho = -divergence(rho, up(rho[t]))
    d_en = -divergence(en, en_hi)
    d_vp = -divergence(vp, up(vp[t])) - 0.5 * ROTATION * vr[t]
    grad_r = 0.5 * GAMMA_LESS * (en_hi - down(en[t]))
    grad_t = 0.5 * GAMMA_LESS * (en[t + 1] - en[t - 1])
    lap_r = vr[t + 1] + vr[t - 1] + vr_hi + down(vr[t]) - 4.0 * vr[t]
    lap_t = vt[t + 1] + vt[t - 1] + up(vt[t]) + down(vt[t]) - 4.0 * vt[t]
    d_vr = -grad_r * inv_rho + 0.5 * DAMPING * lap_r + 2.0 * ROTATION * vp[t]
    d_vt = -grad_t * inv_rho + 0.5 * DAMPING * lap_t
    return d_rho, d_en, d_vr, d_vt, d_vp


def stencil_kernel(own_ref, lo_ref, hi_ref, side_ref, out_ref):
    row = lax.axis_index("row")
    theta = lax.axis_index("theta")
    pos = lax.broadcasted_iota(jnp.int32, (TILE, LANES), 0)
    near = jnp.where(row == 0, pos, TILE - 1 - pos) < TILE // 2

    def own(f, t):
        if t < 2:
            return lo_ref[f, t]
        if t >= TH + 2:
            return hi_ref[f, t - TH - 2]
        return own_ref[f, t - 2]

    def wide(f, t):
        return jnp.concatenate([own(f, t), jnp.where(near, side_ref[f, t], 0.0)], 0)

    field = [[wide(f, t) for t in range(TH + 4)] for f in range(FIELDS)]
    first = [[None] * (TH + 4) for _ in range(FIELDS)]
    side_in = jnp.concatenate([jnp.ones((CR, LANES), jnp.bool_), near], 0)
    inverse = [None] * (TH + 4)
    for t in range(1, TH + 3):
        inside = side_in
        if t == 1:
            inside = side_in & (theta > 0)
        if t == TH + 2:
            inside = side_in & (theta < lax.axis_size("theta") - 1)
        inverse[t] = 1.0 / jnp.where(inside, field[0][t], 1.0)
        steps = rates(field, inverse[t], t)
        for f in range(FIELDS):
            first[f][t] = jnp.where(inside, field[f][t] + TIME_STEP * steps[f], 0.0)
    for t in range(2, TH + 2):
        steps = rates(first, inverse[t], t)
        for f in range(FIELDS):
            second = 0.5 * (field[f][t] + first[f][t] + TIME_STEP * steps[f])
            for p in range(PAIRS):
                start = (t - 2) * TILE * ROWS + f * PAIRS + p
                out_ref[pl.ds(start, TILE, stride=ROWS), :] = second[p * TILE : (p + 1) * TILE]


def rotate_kernel(shift_ref, visc_ref, in_ref, out_ref, twice_ref):
    mine = lax.axis_index("phi") % TILE
    lane = lax.broadcasted_iota(jnp.int32, (PHI, LANES), 1)
    for p in range(PAIRS):
        radius = mine + p * TILE
        shift = shift_ref[radius]
        nu = visc_ref[radius]
        hops = lax.shift_right_logical(shift, 7)
        rest = jnp.bitwise_and(shift, LANES - 1)
        wrapped = lane < rest

        def shifted(f):
            turned = pltpu.roll(in_ref[pl.ds(f * PAIRS + p, PHI, stride=ROWS), :], rest, 1)
            slot = f * PAIRS + p
            twice_ref[slot, :PHI] = turned
            twice_ref[slot, PHI:] = turned
            near = twice_ref[slot, pl.ds(PHI - hops, PHI), :]
            far = twice_ref[slot, pl.ds(PHI - 1 - hops, PHI), :]
            return jnp.where(wrapped, far, near)

        def put(f, value):
            out_ref[pl.ds(f * PAIRS + p, PHI, stride=ROWS), :] = value

        def sides(value):
            right = pltpu.roll(value, 1, 1)
            left = pltpu.roll(value, LANES - 1, 1)
            behind = jnp.where(lane == 0, pltpu.roll(right, 1, 0), right)
            ahead = jnp.where(lane == LANES - 1, pltpu.roll(left, PHI - 1, 0), left)
            return behind, ahead

        rho = shifted(0)
        put(0, rho)
        for f in range(2, FIELDS):
            value = shifted(f)
            behind, ahead = sides(value)
            put(f, value + nu * (ahead - 2.0 * value + behind))
            if f == FIELDS - 1:
                slope = 0.5 * (ahead - behind)
                put(1, shifted(1) + nu * rho * slope * slope)


def unpack_kernel(in_ref, rho_ref, en_ref, vel_ref):
    for f in range(FIELDS):
        for t in range(TH):
            for p in range(PAIRS):
                start = t * TILE * ROWS + f * PAIRS + p
                value = in_ref[pl.ds(start, TILE, stride=ROWS), :]
                span = slice(p * TILE, (p + 1) * TILE)
                if f == 0:
                    rho_ref[t, span] = value
                elif f == 1:
                    en_ref[t, span] = value
                else:
                    vel_ref[f - 2, t, span] = value


def vmem():
    return pl.BlockSpec(memory_space=pltpu.VMEM)


def smem():
    return pl.BlockSpec(memory_space=pltpu.SMEM)


def near(value):
    return pltpu.with_memory_space_constraint(value, pltpu.VMEM)


def per_device(density, energy, velocity, shifts, viscosity):
    thetas = lax.axis_size("theta")
    rows = lax.axis_index("row")
    fields = jnp.concatenate([density[None], energy[None], velocity], 0)
    upward = [(i, i + 1) for i in range(thetas - 1)]
    downward = [(j, i) for i, j in upward]
    lo = lax.ppermute(fields[:, TH - 2 :], "theta", upward)
    hi = lax.ppermute(fields[:, :2], "theta", downward)
    tall = jnp.concatenate([lo, fields, hi], 1)
    edge = jnp.where(rows == 0, tall[:, :, CR - TILE :], tall[:, :, :TILE])
    side = lax.ppermute(edge, "row", [(0, 1), (1, 0)])
    flat = pltpu.VMEM((PHI * ROWS, LANES), jnp.float32)
    second = pl.pallas_call(
        stencil_kernel,
        out_shape=flat,
        in_specs=[vmem()] * 4,
        out_specs=vmem(),
        name="stencil",
    )(near(fields), near(lo), near(hi), near(side))

    def exchange(value):
        value = lax.all_to_all(value.reshape(-1), "phi", 0, 0, tiled=True)
        return value.reshape(PHI * ROWS, LANES)

    turned = pl.pallas_call(
        rotate_kernel,
        out_shape=flat,
        in_specs=[smem(), smem(), vmem()],
        out_specs=vmem(),
        scratch_shapes=[pltpu.VMEM((ROWS, 2 * PHI, LANES), jnp.float32)],
        name="rotate",
    )(shifts, viscosity, near(exchange(second)))
    block = jax.ShapeDtypeStruct(density.shape, jnp.float32)
    return pl.pallas_call(
        unpack_kernel,
        out_shape=(block, block, jax.ShapeDtypeStruct(velocity.shape, jnp.float32)),
        in_specs=[vmem()],
        out_specs=(vmem(), vmem(), vmem()),
        name="unpack",
    )(near(exchange(turned)))


def solution(mesh):
    return jax.shard_map(
        per_device,
        mesh=mesh,
        in_specs=(
            P("theta", "row", "phi"),
            P("theta", "row", "phi"),
            P(None, "theta", "row", "phi"),
            P("row"),
            P("row"),
        ),
        out_specs=(
            P("theta", "row", "phi"),
            P("theta", "row", "phi"),
            P(None, "theta", "row", "phi"),
        ),
        check_vma=False,
    )
```

```python
import jax
import jax.numpy as jnp
from jax import lax
from jax.experimental import pallas as pl
from jax.experimental.pallas import tpu as pltpu
from jax.sharding import PartitionSpec as P

GAMMA_LESS = 0.4
TIME_STEP = 0.4
DAMPING = 1.0
ROTATION = 0.5

FIELDS = 5
TH = 4
CR = 16
LANES = 128
TILE = 8
PHI = 32
PAIRS = TH * CR // PHI
ROWS = FIELDS * PAIRS


def face(q_lo, q_hi, u_lo, u_hi):
    return 0.25 * (u_lo + u_hi) * (q_lo + q_hi) - 0.5 * DAMPING * (q_hi - q_lo)


def up(value):
    return pltpu.roll(value, value.shape[0] - 1, 0)


def down(value):
    return pltpu.roll(value, 1, 0)


def rates(field, inv_rho, t):
    rho, en, vr, vt, vp = (field[f] for f in range(FIELDS))
    vr_hi = up(vr[t])
    out = []

    def divergence(q, q_hi):
        flux = face(q[t], q_hi, vr[t], vr_hi)
        radial = flux - down(flux)
        polar = face(q[t], q[t + 1], vt[t], vt[t + 1]) - face(q[t - 1], q[t], vt[t - 1], vt[t])
        return radial + polar

    en_hi = up(en[t])
    d_rho = -divergence(rho, up(rho[t]))
    d_en = -divergence(en, en_hi)
    d_vp = -divergence(vp, up(vp[t])) - 0.5 * ROTATION * vr[t]
    grad_r = 0.5 * GAMMA_LESS * (en_hi - down(en[t]))
    grad_t = 0.5 * GAMMA_LESS * (en[t + 1] - en[t - 1])
    lap_r = vr[t + 1] + vr[t - 1] + vr_hi + down(vr[t]) - 4.0 * vr[t]
    lap_t = vt[t + 1] + vt[t - 1] + up(vt[t]) + down(vt[t]) - 4.0 * vt[t]
    d_vr = -grad_r * inv_rho + 0.5 * DAMPING * lap_r + 2.0 * ROTATION * vp[t]
    d_vt = -grad_t * inv_rho + 0.5 * DAMPING * lap_t
    return d_rho, d_en, d_vr, d_vt, d_vp


def pack_kernel(rho_ref, en_ref, vel_ref, shift_ref, visc_ref, out_ref, hop_ref, nu_ref, sems):
    copies = [
        pltpu.make_async_copy(shift_ref, hop_ref, sems.at[3]),
        pltpu.make_async_copy(visc_ref, nu_ref, sems.at[4]),
        pltpu.make_async_copy(rho_ref, out_ref.at[0], sems.at[0]),
        pltpu.make_async_copy(en_ref, out_ref.at[1], sems.at[1]),
        pltpu.make_async_copy(vel_ref, out_ref.at[2:], sems.at[2]),
    ]
    for copy in copies:
        copy.start()
    for copy in copies:
        copy.wait()


def stencil_kernel(own_ref, sib_ref, got_ref, passed_ref, out_ref):
    row = lax.axis_index("row")
    theta = lax.axis_index("theta")
    pos = lax.broadcasted_iota(jnp.int32, (TILE, LANES), 0)
    near = jnp.where(row == 0, pos, TILE - 1 - pos) < TILE // 2

    def halo(f, t, low):
        parts = []
        for start, size in ((CR * row, CR), (CR - TILE * row, TILE)):
            span = pl.ds(pl.multiple_of(start, TILE), size)
            got, passed = got_ref[f, t, span, :], passed_ref[f, t, span, :]
            parts.append(jnp.where((row == 0) == low, got, passed))
        return parts

    def wide(f, t):
        if t < 2:
            own, side = halo(f, t, True)
        elif t >= TH + 2:
            own, side = halo(f, t - TH - 2, False)
        else:
            own = own_ref[f, t - 2]
            side = sib_ref[f, t - 2, pl.ds(pl.multiple_of(TILE * row, TILE), TILE), :]
        return jnp.concatenate([own, jnp.where(near, side, 0.0)], 0)

    field = [[wide(f, t) for t in range(TH + 4)] for f in range(FIELDS)]
    first = [[None] * (TH + 4) for _ in range(FIELDS)]
    side_in = jnp.concatenate([jnp.ones((CR, LANES), jnp.bool_), near], 0)
    inverse = [None] * (TH + 4)
    for t in range(1, TH + 3):
        inside = side_in
        if t == 1:
            inside = side_in & (theta > 0)
        if t == TH + 2:
            inside = side_in & (theta < lax.axis_size("theta") - 1)
        inverse[t] = 1.0 / jnp.where(inside, field[0][t], 1.0)
        steps = rates(field, inverse[t], t)
        for f in range(FIELDS):
            first[f][t] = jnp.where(inside, field[f][t] + TIME_STEP * steps[f], 0.0)
    for t in range(2, TH + 2):
        steps = rates(first, inverse[t], t)
        for f in range(FIELDS):
            second = 0.5 * (field[f][t] + first[f][t] + TIME_STEP * steps[f])
            for p in range(PAIRS):
                start = (t - 2) * TILE * ROWS + f * PAIRS + p
                out_ref[pl.ds(start, TILE, stride=ROWS), :] = second[p * TILE : (p + 1) * TILE]


def rotate_kernel(shift_ref, visc_ref, in_ref, out_ref, twice_ref):
    mine = lax.axis_index("phi") % TILE
    lane = lax.broadcasted_iota(jnp.int32, (PHI, LANES), 1)
    for p in range(PAIRS):
        radius = mine + p * TILE
        shift = shift_ref[radius]
        nu = visc_ref[radius]
        hops = lax.shift_right_logical(shift, 7)
        rest = jnp.bitwise_and(shift, LANES - 1)
        wrapped = lane < rest

        def shifted(f):
            turned = pltpu.roll(in_ref[pl.ds(f * PAIRS + p, PHI, stride=ROWS), :], rest, 1)
            slot = f * PAIRS + p
            twice_ref[slot, :PHI] = turned
            twice_ref[slot, PHI:] = turned
            near = twice_ref[slot, pl.ds(PHI - hops, PHI), :]
            far = twice_ref[slot, pl.ds(PHI - 1 - hops, PHI), :]
            return jnp.where(wrapped, far, near)

        def put(f, value):
            out_ref[pl.ds(f * PAIRS + p, PHI, stride=ROWS), :] = value

        def sides(value):
            right = pltpu.roll(value, 1, 1)
            left = pltpu.roll(value, LANES - 1, 1)
            behind = jnp.where(lane == 0, pltpu.roll(right, 1, 0), right)
            ahead = jnp.where(lane == LANES - 1, pltpu.roll(left, PHI - 1, 0), left)
            return behind, ahead

        rho = shifted(0)
        put(0, rho)
        for f in range(2, FIELDS):
            value = shifted(f)
            behind, ahead = sides(value)
            put(f, value + nu * (ahead - 2.0 * value + behind))
            if f == FIELDS - 1:
                slope = 0.5 * (ahead - behind)
                put(1, shifted(1) + nu * rho * slope * slope)


def unpack_kernel(in_ref, rho_ref, en_ref, vel_ref):
    for f in range(FIELDS):
        for t in range(TH):
            for p in range(PAIRS):
                start = t * TILE * ROWS + f * PAIRS + p
                value = in_ref[pl.ds(start, TILE, stride=ROWS), :]
                span = slice(p * TILE, (p + 1) * TILE)
                if f == 0:
                    rho_ref[t, span] = value
                elif f == 1:
                    en_ref[t, span] = value
                else:
                    vel_ref[f - 2, t, span] = value


def vmem():
    return pl.BlockSpec(memory_space=pltpu.VMEM)


def smem():
    return pl.BlockSpec(memory_space=pltpu.SMEM)


def near(value):
    return pltpu.with_memory_space_constraint(value, pltpu.VMEM)


def per_device(density, energy, velocity, shifts, viscosity):
    thetas = lax.axis_size("theta")
    row = lax.axis_index("row")
    swap = [(0, 1), (1, 0)]
    sibling = jnp.concatenate(
        [
            lax.ppermute(density, "row", swap)[None],
            lax.ppermute(energy, "row", swap)[None],
            lax.ppermute(velocity, "row", swap),
        ],
        0,
    )
    fields, hops, nu = pl.pallas_call(
        pack_kernel,
        out_shape=(
            pltpu.VMEM((FIELDS,) + density.shape, jnp.float32),
            pltpu.SMEM(shifts.shape, jnp.int32),
            pltpu.SMEM(viscosity.shape, jnp.float32),
        ),
        in_specs=[pl.BlockSpec(memory_space=pl.ANY)] * 5,
        out_specs=(vmem(), smem(), smem()),
        scratch_shapes=[pltpu.SemaphoreType.DMA((5,))],
        name="pack",
    )(density, energy, velocity, shifts, viscosity)
    outer = jnp.where(
        row == 0,
        jnp.concatenate([fields[:, :2], sibling[:, :2]], 2),
        jnp.concatenate([sibling[:, TH - 2 :], fields[:, TH - 2 :]], 2),
    )
    across = [(thetas + i, i + 1) for i in range(thetas - 1)]
    got = lax.ppermute(outer, ("row", "theta"), across + [(j, i) for i, j in across])
    passed = lax.ppermute(got, "row", swap)
    flat = pltpu.VMEM((PHI * ROWS, LANES), jnp.float32)
    second = pl.pallas_call(
        stencil_kernel,
        out_shape=flat,
        in_specs=[vmem()] * 4,
        out_specs=vmem(),
        name="stencil",
    )(near(fields), near(sibling), near(got), near(passed))

    def exchange(value):
        value = lax.all_to_all(value.reshape(-1), "phi", 0, 0, tiled=True)
        return value.reshape(PHI * ROWS, LANES)

    turned = pl.pallas_call(
        rotate_kernel,
        out_shape=flat,
        in_specs=[smem(), smem(), vmem()],
        out_specs=vmem(),
        scratch_shapes=[pltpu.VMEM((ROWS, 2 * PHI, LANES), jnp.float32)],
        name="rotate",
    )(
        pltpu.with_memory_space_constraint(hops, pltpu.SMEM),
        pltpu.with_memory_space_constraint(nu, pltpu.SMEM),
        near(exchange(second)),
    )
    block = jax.ShapeDtypeStruct(density.shape, jnp.float32)
    return pl.pallas_call(
        unpack_kernel,
        out_shape=(block, block, jax.ShapeDtypeStruct(velocity.shape, jnp.float32)),
        in_specs=[vmem()],
        out_specs=(vmem(), vmem(), vmem()),
        name="unpack",
    )(near(exchange(turned)))


def solution(mesh):
    return jax.shard_map(
        per_device,
        mesh=mesh,
        in_specs=(
            P("theta", "row", "phi"),
            P("theta", "row", "phi"),
            P(None, "theta", "row", "phi"),
            P("row"),
            P("row"),
        ),
        out_specs=(
            P("theta", "row", "phi"),
            P("theta", "row", "phi"),
            P(None, "theta", "row", "phi"),
        ),
        check_vma=False,
    )
```

```python
import jax
import jax.numpy as jnp
from jax import lax
from jax.experimental import pallas as pl
from jax.experimental.pallas import tpu as pltpu
from jax.sharding import PartitionSpec as P

GAMMA_LESS = 0.4
TIME_STEP = 0.4
DAMPING = 1.0
ROTATION = 0.5

FIELDS = 5
TH = 4
CR = 16
LANES = 128
TILE = 8
PHI = 32
PAIRS = TH * CR // PHI
ROWS = FIELDS * PAIRS


def face(q_lo, q_hi, u_lo, u_hi):
    return 0.25 * (u_lo + u_hi) * (q_lo + q_hi) - 0.5 * DAMPING * (q_hi - q_lo)


def up(value):
    return pltpu.roll(value, value.shape[0] - 1, 0)


def down(value):
    return pltpu.roll(value, 1, 0)


def rates(field, inv_rho, t):
    rho, en, vr, vt, vp = (field[f] for f in range(FIELDS))
    vr_hi = up(vr[t])
    out = []

    def divergence(q, q_hi):
        flux = face(q[t], q_hi, vr[t], vr_hi)
        radial = flux - down(flux)
        polar = face(q[t], q[t + 1], vt[t], vt[t + 1]) - face(q[t - 1], q[t], vt[t - 1], vt[t])
        return radial + polar

    en_hi = up(en[t])
    d_rho = -divergence(rho, up(rho[t]))
    d_en = -divergence(en, en_hi)
    d_vp = -divergence(vp, up(vp[t])) - 0.5 * ROTATION * vr[t]
    grad_r = 0.5 * GAMMA_LESS * (en_hi - down(en[t]))
    grad_t = 0.5 * GAMMA_LESS * (en[t + 1] - en[t - 1])
    lap_r = vr[t + 1] + vr[t - 1] + vr_hi + down(vr[t]) - 4.0 * vr[t]
    lap_t = vt[t + 1] + vt[t - 1] + up(vt[t]) + down(vt[t]) - 4.0 * vt[t]
    d_vr = -grad_r * inv_rho + 0.5 * DAMPING * lap_r + 2.0 * ROTATION * vp[t]
    d_vt = -grad_t * inv_rho + 0.5 * DAMPING * lap_t
    return d_rho, d_en, d_vr, d_vt, d_vp


def pack_kernel(rho_ref, en_ref, vel_ref, shift_ref, visc_ref, out_ref, hop_ref, nu_ref, sems):
    copies = [
        pltpu.make_async_copy(shift_ref, hop_ref, sems.at[3]),
        pltpu.make_async_copy(visc_ref, nu_ref, sems.at[4]),
        pltpu.make_async_copy(rho_ref, out_ref.at[0], sems.at[0]),
        pltpu.make_async_copy(en_ref, out_ref.at[1], sems.at[1]),
        pltpu.make_async_copy(vel_ref, out_ref.at[2:], sems.at[2]),
    ]
    for copy in copies:
        copy.start()
    for copy in copies:
        copy.wait()


def stencil_kernel(own_ref, sib_ref, got_ref, passed_ref, out_ref):
    row = lax.axis_index("row")
    theta = lax.axis_index("theta")
    pos = lax.broadcasted_iota(jnp.int32, (TILE, LANES), 0)
    near = jnp.where(row == 0, pos, TILE - 1 - pos) < TILE // 2

    def halo(f, t, low):
        parts = []
        for start, size in ((CR * row, CR), (CR - TILE * row, TILE)):
            span = pl.ds(pl.multiple_of(start, TILE), size)
            got, passed = got_ref[f, t, span, :], passed_ref[f, t, span, :]
            parts.append(jnp.where((row == 0) == low, got, passed))
        return parts

    near = jnp.concatenate([jnp.ones((CR, LANES), jnp.bool_), near], 0)
    below = near & (theta > 0)
    above = near & (theta < lax.axis_size("theta") - 1)

    def wide(f, t):
        if t < 2:
            inside, parts = below, halo(f, t, True)
        elif t >= TH + 2:
            inside, parts = above, halo(f, t - TH - 2, False)
        else:
            side = sib_ref[f, t - 2, pl.ds(pl.multiple_of(TILE * row, TILE), TILE), :]
            inside, parts = near, [own_ref[f, t - 2], side]
        return jnp.where(inside, jnp.concatenate(parts, 0), 0.0)

    field = [[wide(f, t) for t in range(TH + 4)] for f in range(FIELDS)]
    first = [[None] * (TH + 4) for _ in range(FIELDS)]
    inverse = [None] * (TH + 4)
    for t in range(1, TH + 3):
        inside = below if t == 1 else above if t == TH + 2 else near
        inverse[t] = 1.0 / jnp.where(inside, field[0][t], 1.0)
        steps = rates(field, inverse[t], t)
        for f in range(FIELDS):
            first[f][t] = jnp.where(inside, field[f][t] + TIME_STEP * steps[f], 0.0)
    for t in range(2, TH + 2):
        steps = rates(first, inverse[t], t)
        for f in range(FIELDS):
            second = 0.5 * (field[f][t] + first[f][t] + TIME_STEP * steps[f])
            for p in range(PAIRS):
                start = (t - 2) * TILE * ROWS + f * PAIRS + p
                out_ref[pl.ds(start, TILE, stride=ROWS), :] = second[p * TILE : (p + 1) * TILE]


def rotate_kernel(shift_ref, visc_ref, in_ref, out_ref, twice_ref):
    mine = lax.axis_index("phi") % TILE
    lane = lax.broadcasted_iota(jnp.int32, (PHI, LANES), 1)
    for p in range(PAIRS):
        radius = mine + p * TILE
        shift = shift_ref[radius]
        nu = visc_ref[radius]
        hops = lax.shift_right_logical(shift, 7)
        rest = jnp.bitwise_and(shift, LANES - 1)
        wrapped = lane < rest

        def shifted(f):
            turned = pltpu.roll(in_ref[pl.ds(f * PAIRS + p, PHI, stride=ROWS), :], rest, 1)
            slot = f * PAIRS + p
            twice_ref[slot, :PHI] = turned
            twice_ref[slot, PHI:] = turned
            near = twice_ref[slot, pl.ds(PHI - hops, PHI), :]
            far = twice_ref[slot, pl.ds(PHI - 1 - hops, PHI), :]
            return jnp.where(wrapped, far, near)

        def put(f, value):
            out_ref[pl.ds(f * PAIRS + p, PHI, stride=ROWS), :] = value

        def sides(value):
            right = pltpu.roll(value, 1, 1)
            left = pltpu.roll(value, LANES - 1, 1)
            behind = jnp.where(lane == 0, pltpu.roll(right, 1, 0), right)
            ahead = jnp.where(lane == LANES - 1, pltpu.roll(left, PHI - 1, 0), left)
            return behind, ahead

        rho = shifted(0)
        put(0, rho)
        for f in range(2, FIELDS):
            value = shifted(f)
            behind, ahead = sides(value)
            put(f, value + nu * (ahead - 2.0 * value + behind))
            if f == FIELDS - 1:
                slope = 0.5 * (ahead - behind)
                put(1, shifted(1) + nu * rho * slope * slope)


def unpack_kernel(in_ref, rho_ref, en_ref, vel_ref):
    for f in range(FIELDS):
        for t in range(TH):
            for p in range(PAIRS):
                start = t * TILE * ROWS + f * PAIRS + p
                value = in_ref[pl.ds(start, TILE, stride=ROWS), :]
                span = slice(p * TILE, (p + 1) * TILE)
                if f == 0:
                    rho_ref[t, span] = value
                elif f == 1:
                    en_ref[t, span] = value
                else:
                    vel_ref[f - 2, t, span] = value


def vmem():
    return pl.BlockSpec(memory_space=pltpu.VMEM)


def smem():
    return pl.BlockSpec(memory_space=pltpu.SMEM)


def near(value):
    return pltpu.with_memory_space_constraint(value, pltpu.VMEM)


def per_device(density, energy, velocity, shifts, viscosity):
    thetas = lax.axis_size("theta")
    row = lax.axis_index("row")
    swap = [(0, 1), (1, 0)]
    sibling = jnp.concatenate(
        [
            lax.ppermute(density, "row", swap)[None],
            lax.ppermute(energy, "row", swap)[None],
            lax.ppermute(velocity, "row", swap),
        ],
        0,
    )
    fields, hops, nu = pl.pallas_call(
        pack_kernel,
        out_shape=(
            pltpu.VMEM((FIELDS,) + density.shape, jnp.float32),
            pltpu.SMEM(shifts.shape, jnp.int32),
            pltpu.SMEM(viscosity.shape, jnp.float32),
        ),
        in_specs=[pl.BlockSpec(memory_space=pl.ANY)] * 5,
        out_specs=(vmem(), smem(), smem()),
        scratch_shapes=[pltpu.SemaphoreType.DMA((5,))],
        name="pack",
    )(density, energy, velocity, shifts, viscosity)
    outer = jnp.where(
        row == 0,
        jnp.concatenate([fields[:, :2], sibling[:, :2]], 2),
        jnp.concatenate([sibling[:, TH - 2 :], fields[:, TH - 2 :]], 2),
    )
    across = [(thetas + i, (i + 1) % thetas) for i in range(thetas)]
    got = lax.ppermute(outer, ("row", "theta"), across + [(j, i) for i, j in across])
    passed = lax.ppermute(got, "row", swap)
    flat = pltpu.VMEM((PHI * ROWS, LANES), jnp.float32)
    second = pl.pallas_call(
        stencil_kernel,
        out_shape=flat,
        in_specs=[vmem()] * 4,
        out_specs=vmem(),
        name="stencil",
    )(near(fields), near(sibling), near(got), near(passed))

    def exchange(value):
        value = lax.all_to_all(value.reshape(-1), "phi", 0, 0, tiled=True)
        return value.reshape(PHI * ROWS, LANES)

    turned = pl.pallas_call(
        rotate_kernel,
        out_shape=flat,
        in_specs=[smem(), smem(), vmem()],
        out_specs=vmem(),
        scratch_shapes=[pltpu.VMEM((ROWS, 2 * PHI, LANES), jnp.float32)],
        name="rotate",
    )(
        pltpu.with_memory_space_constraint(hops, pltpu.SMEM),
        pltpu.with_memory_space_constraint(nu, pltpu.SMEM),
        near(exchange(second)),
    )
    block = jax.ShapeDtypeStruct(density.shape, jnp.float32)
    return pl.pallas_call(
        unpack_kernel,
        out_shape=(block, block, jax.ShapeDtypeStruct(velocity.shape, jnp.float32)),
        in_specs=[vmem()],
        out_specs=(vmem(), vmem(), vmem()),
        name="unpack",
    )(near(exchange(turned)))


def solution(mesh):
    return jax.shard_map(
        per_device,
        mesh=mesh,
        in_specs=(
            P("theta", "row", "phi"),
            P("theta", "row", "phi"),
            P(None, "theta", "row", "phi"),
            P("row"),
            P("row"),
        ),
        out_specs=(
            P("theta", "row", "phi"),
            P("theta", "row", "phi"),
            P(None, "theta", "row", "phi"),
        ),
        check_vma=False,
    )
```

```python
import jax
import jax.numpy as jnp
from jax import lax
from jax.experimental import pallas as pl
from jax.experimental.pallas import tpu as pltpu
from jax.sharding import PartitionSpec as P

GAMMA_LESS = 0.4
TIME_STEP = 0.4
DAMPING = 1.0
ROTATION = 0.5

FIELDS = 5
TH = 4
CR = 16
LANES = 128
TILE = 8
PHI = 32
PAIRS = TH * CR // PHI
ROWS = FIELDS * PAIRS


def face(q_lo, q_hi, u_lo, u_hi):
    return 0.25 * (u_lo + u_hi) * (q_lo + q_hi) - 0.5 * DAMPING * (q_hi - q_lo)


def up(value):
    return pltpu.roll(value, value.shape[0] - 1, 0)


def down(value):
    return pltpu.roll(value, 1, 0)


def rates(field, inv_rho, t):
    rho, en, vr, vt, vp = (field[f] for f in range(FIELDS))
    vr_hi = up(vr[t])
    out = []

    def divergence(q, q_hi):
        flux = face(q[t], q_hi, vr[t], vr_hi)
        radial = flux - down(flux)
        polar = face(q[t], q[t + 1], vt[t], vt[t + 1]) - face(q[t - 1], q[t], vt[t - 1], vt[t])
        return radial + polar

    en_hi = up(en[t])
    d_rho = -divergence(rho, up(rho[t]))
    d_en = -divergence(en, en_hi)
    d_vp = -divergence(vp, up(vp[t])) - 0.5 * ROTATION * vr[t]
    grad_r = 0.5 * GAMMA_LESS * (en_hi - down(en[t]))
    grad_t = 0.5 * GAMMA_LESS * (en[t + 1] - en[t - 1])
    lap_r = vr[t + 1] + vr[t - 1] + vr_hi + down(vr[t]) - 4.0 * vr[t]
    lap_t = vt[t + 1] + vt[t - 1] + up(vt[t]) + down(vt[t]) - 4.0 * vt[t]
    d_vr = -grad_r * inv_rho + 0.5 * DAMPING * lap_r + 2.0 * ROTATION * vp[t]
    d_vt = -grad_t * inv_rho + 0.5 * DAMPING * lap_t
    return d_rho, d_en, d_vr, d_vt, d_vp


def pack_kernel(rho_ref, en_ref, vel_ref, shift_ref, visc_ref, out_ref, hop_ref, nu_ref, sems):
    copies = [
        pltpu.make_async_copy(shift_ref, hop_ref, sems.at[3]),
        pltpu.make_async_copy(visc_ref, nu_ref, sems.at[4]),
        pltpu.make_async_copy(rho_ref, out_ref.at[0], sems.at[0]),
        pltpu.make_async_copy(en_ref, out_ref.at[1], sems.at[1]),
        pltpu.make_async_copy(vel_ref, out_ref.at[2:], sems.at[2]),
    ]
    for copy in copies:
        copy.start()
    for copy in copies:
        copy.wait()


def stencil_kernel(own_ref, lo_ref, hi_ref, side_ref, out_ref):
    row = lax.axis_index("row")
    theta = lax.axis_index("theta")
    pos = lax.broadcasted_iota(jnp.int32, (TILE, LANES), 0)
    near = jnp.where(row == 0, pos, TILE - 1 - pos) < TILE // 2
    near = jnp.concatenate([jnp.ones((CR, LANES), jnp.bool_), near], 0)
    below = near & (theta > 0)
    above = near & (theta < lax.axis_size("theta") - 1)

    def wide(f, t):
        if t < 2:
            inside, own = below, lo_ref[f, t]
        elif t >= TH + 2:
            inside, own = above, hi_ref[f, t - TH - 2]
        else:
            inside, own = near, own_ref[f, t - 2]
        return jnp.where(inside, jnp.concatenate([own, side_ref[f, t]], 0), 0.0)

    field = [[wide(f, t) for t in range(TH + 4)] for f in range(FIELDS)]
    first = [[None] * (TH + 4) for _ in range(FIELDS)]
    inverse = [None] * (TH + 4)
    for t in range(1, TH + 3):
        inside = below if t == 1 else above if t == TH + 2 else near
        inverse[t] = 1.0 / jnp.where(inside, field[0][t], 1.0)
        steps = rates(field, inverse[t], t)
        for f in range(FIELDS):
            first[f][t] = jnp.where(inside, field[f][t] + TIME_STEP * steps[f], 0.0)
    for t in range(2, TH + 2):
        steps = rates(first, inverse[t], t)
        for f in range(FIELDS):
            second = 0.5 * (field[f][t] + first[f][t] + TIME_STEP * steps[f])
            for p in range(PAIRS):
                start = (t - 2) * TILE * ROWS + f * PAIRS + p
                out_ref[pl.ds(start, TILE, stride=ROWS), :] = second[p * TILE : (p + 1) * TILE]


def rotate_kernel(shift_ref, visc_ref, in_ref, out_ref, twice_ref):
    mine = lax.axis_index("phi") % TILE
    lane = lax.broadcasted_iota(jnp.int32, (PHI, LANES), 1)
    for p in range(PAIRS):
        radius = mine + p * TILE
        shift = shift_ref[radius]
        nu = visc_ref[radius]
        hops = lax.shift_right_logical(shift, 7)
        rest = jnp.bitwise_and(shift, LANES - 1)
        wrapped = lane < rest

        def shifted(f):
            turned = pltpu.roll(in_ref[pl.ds(f * PAIRS + p, PHI, stride=ROWS), :], rest, 1)
            slot = f * PAIRS + p
            twice_ref[slot, :PHI] = turned
            twice_ref[slot, PHI:] = turned
            near = twice_ref[slot, pl.ds(PHI - hops, PHI), :]
            far = twice_ref[slot, pl.ds(PHI - 1 - hops, PHI), :]
            return jnp.where(wrapped, far, near)

        def put(f, value):
            out_ref[pl.ds(f * PAIRS + p, PHI, stride=ROWS), :] = value

        def sides(value):
            right = pltpu.roll(value, 1, 1)
            left = pltpu.roll(value, LANES - 1, 1)
            behind = jnp.where(lane == 0, pltpu.roll(right, 1, 0), right)
            ahead = jnp.where(lane == LANES - 1, pltpu.roll(left, PHI - 1, 0), left)
            return behind, ahead

        rho = shifted(0)
        put(0, rho)
        for f in range(2, FIELDS):
            value = shifted(f)
            behind, ahead = sides(value)
            put(f, value + nu * (ahead - 2.0 * value + behind))
            if f == FIELDS - 1:
                slope = 0.5 * (ahead - behind)
                put(1, shifted(1) + nu * rho * slope * slope)


def unpack_kernel(in_ref, rho_ref, en_ref, vel_ref):
    for f in range(FIELDS):
        for t in range(TH):
            for p in range(PAIRS):
                start = t * TILE * ROWS + f * PAIRS + p
                value = in_ref[pl.ds(start, TILE, stride=ROWS), :]
                span = slice(p * TILE, (p + 1) * TILE)
                if f == 0:
                    rho_ref[t, span] = value
                elif f == 1:
                    en_ref[t, span] = value
                else:
                    vel_ref[f - 2, t, span] = value


def vmem():
    return pl.BlockSpec(memory_space=pltpu.VMEM)


def smem():
    return pl.BlockSpec(memory_space=pltpu.SMEM)


def near(value):
    return pltpu.with_memory_space_constraint(value, pltpu.VMEM)


def per_device(density, energy, velocity, shifts, viscosity):
    thetas = lax.axis_size("theta")
    row = lax.axis_index("row")
    fields, hops, nu = pl.pallas_call(
        pack_kernel,
        out_shape=(
            pltpu.VMEM((FIELDS,) + density.shape, jnp.float32),
            pltpu.SMEM(shifts.shape, jnp.int32),
            pltpu.SMEM(viscosity.shape, jnp.float32),
        ),
        in_specs=[pl.BlockSpec(memory_space=pl.ANY)] * 5,
        out_specs=(vmem(), smem(), smem()),
        scratch_shapes=[pltpu.SemaphoreType.DMA((5,))],
        name="pack",
    )(density, energy, velocity, shifts, viscosity)
    upward = [(i, (i + 1) % thetas) for i in range(thetas)]
    downward = [(j, i) for i, j in upward]
    lo = lax.ppermute(fields[:, TH - 2 :], "theta", upward)
    hi = lax.ppermute(fields[:, :2], "theta", downward)
    tall = jnp.concatenate([lo, fields, hi], 1)
    edge = jnp.where(row == 0, tall[:, :, CR - TILE :], tall[:, :, :TILE])
    side = lax.ppermute(edge, "row", [(0, 1), (1, 0)])
    flat = pltpu.VMEM((PHI * ROWS, LANES), jnp.float32)
    second = pl.pallas_call(
        stencil_kernel,
        out_shape=flat,
        in_specs=[vmem()] * 4,
        out_specs=vmem(),
        name="stencil",
    )(near(fields), near(lo), near(hi), near(side))

    def exchange(value):
        value = lax.all_to_all(value.reshape(-1), "phi", 0, 0, tiled=True)
        return value.reshape(PHI * ROWS, LANES)

    turned = pl.pallas_call(
        rotate_kernel,
        out_shape=flat,
        in_specs=[smem(), smem(), vmem()],
        out_specs=vmem(),
        scratch_shapes=[pltpu.VMEM((ROWS, 2 * PHI, LANES), jnp.float32)],
        name="rotate",
    )(
        pltpu.with_memory_space_constraint(hops, pltpu.SMEM),
        pltpu.with_memory_space_constraint(nu, pltpu.SMEM),
        near(exchange(second)),
    )
    block = jax.ShapeDtypeStruct(density.shape, jnp.float32)
    return pl.pallas_call(
        unpack_kernel,
        out_shape=(block, block, jax.ShapeDtypeStruct(velocity.shape, jnp.float32)),
        in_specs=[vmem()],
        out_specs=(vmem(), vmem(), vmem()),
        name="unpack",
    )(near(exchange(turned)))


def solution(mesh):
    return jax.shard_map(
        per_device,
        mesh=mesh,
        in_specs=(
            P("theta", "row", "phi"),
            P("theta", "row", "phi"),
            P(None, "theta", "row", "phi"),
            P("row"),
            P("row"),
        ),
        out_specs=(
            P("theta", "row", "phi"),
            P("theta", "row", "phi"),
            P(None, "theta", "row", "phi"),
        ),
        check_vma=False,
    )
```

```python
import jax
import jax.numpy as jnp
from jax import lax
from jax.experimental import pallas as pl
from jax.experimental.pallas import tpu as pltpu
from jax.sharding import PartitionSpec as P

GAMMA_LESS = 0.4
TIME_STEP = 0.4
DAMPING = 1.0
ROTATION = 0.5

FIELDS = 5
TH = 4
CR = 16
LANES = 128
TILE = 8
PHI = 32
PAIRS = TH * CR // PHI
ROWS = FIELDS * PAIRS


def face(q_lo, q_hi, u_lo, u_hi):
    return 0.25 * (u_lo + u_hi) * (q_lo + q_hi) - 0.5 * DAMPING * (q_hi - q_lo)


def up(value):
    return pltpu.roll(value, value.shape[0] - 1, 0)


def down(value):
    return pltpu.roll(value, 1, 0)


def rates(field, inv_rho, t):
    rho, en, vr, vt, vp = (field[f] for f in range(FIELDS))
    vr_hi = up(vr[t])
    out = []

    def divergence(q, q_hi):
        flux = face(q[t], q_hi, vr[t], vr_hi)
        radial = flux - down(flux)
        polar = face(q[t], q[t + 1], vt[t], vt[t + 1]) - face(q[t - 1], q[t], vt[t - 1], vt[t])
        return radial + polar

    en_hi = up(en[t])
    d_rho = -divergence(rho, up(rho[t]))
    d_en = -divergence(en, en_hi)
    d_vp = -divergence(vp, up(vp[t])) - 0.5 * ROTATION * vr[t]
    grad_r = 0.5 * GAMMA_LESS * (en_hi - down(en[t]))
    grad_t = 0.5 * GAMMA_LESS * (en[t + 1] - en[t - 1])
    lap_r = vr[t + 1] + vr[t - 1] + vr_hi + down(vr[t]) - 4.0 * vr[t]
    lap_t = vt[t + 1] + vt[t - 1] + up(vt[t]) + down(vt[t]) - 4.0 * vt[t]
    d_vr = -grad_r * inv_rho + 0.5 * DAMPING * lap_r + 2.0 * ROTATION * vp[t]
    d_vt = -grad_t * inv_rho + 0.5 * DAMPING * lap_t
    return d_rho, d_en, d_vr, d_vt, d_vp


def pack_kernel(rho_ref, en_ref, vel_ref, shift_ref, visc_ref, out_ref, hop_ref, nu_ref, sems):
    copies = [
        pltpu.make_async_copy(shift_ref, hop_ref, sems.at[3]),
        pltpu.make_async_copy(visc_ref, nu_ref, sems.at[4]),
        pltpu.make_async_copy(rho_ref, out_ref.at[0], sems.at[0]),
        pltpu.make_async_copy(en_ref, out_ref.at[1], sems.at[1]),
        pltpu.make_async_copy(vel_ref, out_ref.at[2:], sems.at[2]),
    ]
    for copy in copies:
        copy.start()
    for copy in copies:
        copy.wait()


def stencil_kernel(own_ref, lo_ref, hi_ref, side_ref, out_ref):
    row = lax.axis_index("row")
    theta = lax.axis_index("theta")
    pos = lax.broadcasted_iota(jnp.int32, (TILE, LANES), 0)
    first_pos = jnp.where(row == 0, 0, TILE - 2)
    at_first, at_second = pos == first_pos, pos == first_pos + 1
    near = at_first | at_second
    near = jnp.concatenate([jnp.ones((CR, LANES), jnp.bool_), near], 0)
    below = near & (theta > 0)
    above = near & (theta < lax.axis_size("theta") - 1)

    def wide(f, t):
        if t < 2:
            inside, own = below, lo_ref[f, t]
        elif t >= TH + 2:
            inside, own = above, hi_ref[f, t - TH - 2]
        else:
            inside, own = near, own_ref[f, t - 2]
        one = jnp.broadcast_to(side_ref[f, t, :1], (TILE, LANES))
        two = jnp.broadcast_to(side_ref[f, t, 1:], (TILE, LANES))
        return jnp.where(inside, jnp.concatenate([own, jnp.where(at_first, one, two)], 0), 0.0)

    field = [[wide(f, t) for t in range(TH + 4)] for f in range(FIELDS)]
    first = [[None] * (TH + 4) for _ in range(FIELDS)]
    inverse = [None] * (TH + 4)
    for t in range(1, TH + 3):
        inside = below if t == 1 else above if t == TH + 2 else near
        inverse[t] = 1.0 / jnp.where(inside, field[0][t], 1.0)
        steps = rates(field, inverse[t], t)
        for f in range(FIELDS):
            first[f][t] = jnp.where(inside, field[f][t] + TIME_STEP * steps[f], 0.0)
    for t in range(2, TH + 2):
        steps = rates(first, inverse[t], t)
        for f in range(FIELDS):
            second = 0.5 * (field[f][t] + first[f][t] + TIME_STEP * steps[f])
            for p in range(PAIRS):
                start = (t - 2) * TILE * ROWS + f * PAIRS + p
                out_ref[pl.ds(start, TILE, stride=ROWS), :] = second[p * TILE : (p + 1) * TILE]


def rotate_kernel(shift_ref, visc_ref, in_ref, out_ref, twice_ref):
    mine = lax.axis_index("phi") % TILE
    lane = lax.broadcasted_iota(jnp.int32, (PHI, LANES), 1)
    for p in range(PAIRS):
        radius = mine + p * TILE
        shift = shift_ref[radius]
        nu = visc_ref[radius]
        hops = lax.shift_right_logical(shift, 7)
        rest = jnp.bitwise_and(shift, LANES - 1)
        wrapped = lane < rest

        def shifted(f):
            turned = pltpu.roll(in_ref[pl.ds(f * PAIRS + p, PHI, stride=ROWS), :], rest, 1)
            slot = f * PAIRS + p
            twice_ref[slot, :PHI] = turned
            twice_ref[slot, PHI:] = turned
            near = twice_ref[slot, pl.ds(PHI - hops, PHI), :]
            far = twice_ref[slot, pl.ds(PHI - 1 - hops, PHI), :]
            return jnp.where(wrapped, far, near)

        def put(f, value):
            out_ref[pl.ds(f * PAIRS + p, PHI, stride=ROWS), :] = value

        def sides(value):
            right = pltpu.roll(value, 1, 1)
            left = pltpu.roll(value, LANES - 1, 1)
            behind = jnp.where(lane == 0, pltpu.roll(right, 1, 0), right)
            ahead = jnp.where(lane == LANES - 1, pltpu.roll(left, PHI - 1, 0), left)
            return behind, ahead

        rho = shifted(0)
        put(0, rho)
        for f in range(2, FIELDS):
            value = shifted(f)
            behind, ahead = sides(value)
            put(f, value + nu * (ahead - 2.0 * value + behind))
            if f == FIELDS - 1:
                slope = 0.5 * (ahead - behind)
                put(1, shifted(1) + nu * rho * slope * slope)


def unpack_kernel(in_ref, rho_ref, en_ref, vel_ref):
    for f in range(FIELDS):
        for t in range(TH):
            for p in range(PAIRS):
                start = t * TILE * ROWS + f * PAIRS + p
                value = in_ref[pl.ds(start, TILE, stride=ROWS), :]
                span = slice(p * TILE, (p + 1) * TILE)
                if f == 0:
                    rho_ref[t, span] = value
                elif f == 1:
                    en_ref[t, span] = value
                else:
                    vel_ref[f - 2, t, span] = value


def vmem():
    return pl.BlockSpec(memory_space=pltpu.VMEM)


def smem():
    return pl.BlockSpec(memory_space=pltpu.SMEM)


def near(value):
    return pltpu.with_memory_space_constraint(value, pltpu.VMEM)


def per_device(density, energy, velocity, shifts, viscosity):
    thetas = lax.axis_size("theta")
    row = lax.axis_index("row")
    fields, hops, nu = pl.pallas_call(
        pack_kernel,
        out_shape=(
            pltpu.VMEM((FIELDS,) + density.shape, jnp.float32),
            pltpu.SMEM(shifts.shape, jnp.int32),
            pltpu.SMEM(viscosity.shape, jnp.float32),
        ),
        in_specs=[pl.BlockSpec(memory_space=pl.ANY)] * 5,
        out_specs=(vmem(), smem(), smem()),
        scratch_shapes=[pltpu.SemaphoreType.DMA((5,))],
        name="pack",
    )(density, energy, velocity, shifts, viscosity)
    upward = [(i, (i + 1) % thetas) for i in range(thetas)]
    downward = [(j, i) for i, j in upward]
    lo = lax.ppermute(fields[:, TH - 2 :], "theta", upward)
    hi = lax.ppermute(fields[:, :2], "theta", downward)
    tall = jnp.concatenate([lo, fields, hi], 1)
    edge = jnp.where(row == 0, tall[:, :, CR - 2 :], tall[:, :, :2])
    side = lax.ppermute(edge, "row", [(0, 1), (1, 0)])
    flat = pltpu.VMEM((PHI * ROWS, LANES), jnp.float32)
    second = pl.pallas_call(
        stencil_kernel,
        out_shape=flat,
        in_specs=[vmem()] * 4,
        out_specs=vmem(),
        name="stencil",
    )(near(fields), near(lo), near(hi), near(side))

    def exchange(value):
        value = lax.all_to_all(value.reshape(-1), "phi", 0, 0, tiled=True)
        return value.reshape(PHI * ROWS, LANES)

    turned = pl.pallas_call(
        rotate_kernel,
        out_shape=flat,
        in_specs=[smem(), smem(), vmem()],
        out_specs=vmem(),
        scratch_shapes=[pltpu.VMEM((ROWS, 2 * PHI, LANES), jnp.float32)],
        name="rotate",
    )(
        pltpu.with_memory_space_constraint(hops, pltpu.SMEM),
        pltpu.with_memory_space_constraint(nu, pltpu.SMEM),
        near(exchange(second)),
    )
    block = jax.ShapeDtypeStruct(density.shape, jnp.float32)
    return pl.pallas_call(
        unpack_kernel,
        out_shape=(block, block, jax.ShapeDtypeStruct(velocity.shape, jnp.float32)),
        in_specs=[vmem()],
        out_specs=(vmem(), vmem(), vmem()),
        name="unpack",
    )(near(exchange(turned)))


def solution(mesh):
    return jax.shard_map(
        per_device,
        mesh=mesh,
        in_specs=(
            P("theta", "row", "phi"),
            P("theta", "row", "phi"),
            P(None, "theta", "row", "phi"),
            P("row"),
            P("row"),
        ),
        out_specs=(
            P("theta", "row", "phi"),
            P("theta", "row", "phi"),
            P(None, "theta", "row", "phi"),
        ),
        check_vma=False,
    )
```

```python
import jax
import jax.numpy as jnp
from jax import lax
from jax.experimental import pallas as pl
from jax.experimental.pallas import tpu as pltpu
from jax.sharding import PartitionSpec as P

GAMMA_LESS = 0.4
TIME_STEP = 0.4
DAMPING = 1.0
ROTATION = 0.5

FIELDS = 5
TH = 4
CR = 16
LANES = 128
TILE = 8
PHI = 32
PAIRS = TH * CR // PHI
ROWS = FIELDS * PAIRS
BODY = FIELDS * 2 * CR


def face(q_lo, q_hi, u_lo, u_hi):
    return 0.25 * (u_lo + u_hi) * (q_lo + q_hi) - 0.5 * DAMPING * (q_hi - q_lo)


def up(value):
    return pltpu.roll(value, value.shape[0] - 1, 0)


def down(value):
    return pltpu.roll(value, 1, 0)


def rates(field, inv_rho, t):
    rho, en, vr, vt, vp = (field[f] for f in range(FIELDS))
    vr_hi = up(vr[t])
    out = []

    def divergence(q, q_hi):
        flux = face(q[t], q_hi, vr[t], vr_hi)
        radial = flux - down(flux)
        polar = face(q[t], q[t + 1], vt[t], vt[t + 1]) - face(q[t - 1], q[t], vt[t - 1], vt[t])
        return radial + polar

    en_hi = up(en[t])
    d_rho = -divergence(rho, up(rho[t]))
    d_en = -divergence(en, en_hi)
    d_vp = -divergence(vp, up(vp[t])) - 0.5 * ROTATION * vr[t]
    grad_r = 0.5 * GAMMA_LESS * (en_hi - down(en[t]))
    grad_t = 0.5 * GAMMA_LESS * (en[t + 1] - en[t - 1])
    lap_r = vr[t + 1] + vr[t - 1] + vr_hi + down(vr[t]) - 4.0 * vr[t]
    lap_t = vt[t + 1] + vt[t - 1] + up(vt[t]) + down(vt[t]) - 4.0 * vt[t]
    d_vr = -grad_r * inv_rho + 0.5 * DAMPING * lap_r + 2.0 * ROTATION * vp[t]
    d_vt = -grad_t * inv_rho + 0.5 * DAMPING * lap_t
    return d_rho, d_en, d_vr, d_vt, d_vp


def pack_kernel(rho_ref, en_ref, vel_ref, shift_ref, visc_ref, out_ref, hop_ref, nu_ref, sems):
    copies = [
        pltpu.make_async_copy(shift_ref, hop_ref, sems.at[3]),
        pltpu.make_async_copy(visc_ref, nu_ref, sems.at[4]),
        pltpu.make_async_copy(rho_ref, out_ref.at[0], sems.at[0]),
        pltpu.make_async_copy(en_ref, out_ref.at[1], sems.at[1]),
        pltpu.make_async_copy(vel_ref, out_ref.at[2:], sems.at[2]),
    ]
    for copy in copies:
        copy.start()
    for copy in copies:
        copy.wait()


def side_of(refs, f, t):
    return refs[0].at[t] if f == 0 else refs[1].at[t] if f == 1 else refs[2].at[f - 2, t]


def build_kernel(own_ref, sib_rho, sib_en, sib_vel, up_ref, down_ref):
    border = (CR - 1) * lax.axis_index("row")
    sib = (sib_rho, sib_en, sib_vel)
    for out_ref, low, corner in ((up_ref, TH - 2, TH - 1), (down_ref, 0, 0)):
        out_ref[BODY:] = jnp.zeros((TILE, LANES), jnp.float32)
        for f in range(FIELDS):
            for t in range(2):
                out_ref[(2 * f + t) * CR : (2 * f + t + 1) * CR] = own_ref[f, low + t]
            out_ref[BODY + f : BODY + f + 1] = side_of(sib, f, corner)[pl.ds(border, 1), :]


def stencil_kernel(own_ref, sib_rho, sib_en, sib_vel, lo_ref, hi_ref, out_ref):
    row = lax.axis_index("row")
    theta = lax.axis_index("theta")
    sib = (sib_rho, sib_en, sib_vel)
    pos = lax.broadcasted_iota(jnp.int32, (TILE, LANES), 0)
    first_pos = (TILE - 2) * row
    at_first, at_second = pos == first_pos, pos == first_pos + 1
    at_border = pos == (TILE - 1) * row
    near = jnp.concatenate([jnp.ones((CR, LANES), jnp.bool_), at_border], 0)
    below = near & (theta > 0)
    above = near & (theta < lax.axis_size("theta") - 1)
    nothing = jnp.zeros((TILE, LANES), jnp.float32)

    def spread(line):
        return jnp.broadcast_to(line, (TILE, LANES))

    def wide(f, t):
        if 2 <= t < TH + 2:
            side = side_of(sib, f, t - 2)
            one = spread(side[pl.ds((CR - 2) * row, 1), :])
            two = spread(side[pl.ds((CR - 2) * row + 1, 1), :])
            tile = jnp.where(at_first, one, jnp.where(at_second, two, nothing))
            return jnp.concatenate([own_ref[f, t - 2], tile], 0)
        ref, inside = (lo_ref, below) if t < 2 else (hi_ref, above)
        start = (2 * f + t % 2) * CR
        tile = nothing
        if t in (1, TH + 2):
            tile = spread(ref[BODY + f : BODY + f + 1])
        return jnp.where(inside, jnp.concatenate([ref[start : start + CR], tile], 0), 0.0)

    field = [[wide(f, t) for t in range(TH + 4)] for f in range(FIELDS)]
    first = [[None] * (TH + 4) for _ in range(FIELDS)]
    inverse = [None] * (TH + 4)
    for t in range(1, TH + 3):
        inside = below if t == 1 else above if t == TH + 2 else near
        inverse[t] = 1.0 / jnp.where(inside, field[0][t], 1.0)
        steps = rates(field, inverse[t], t)
        for f in range(FIELDS):
            first[f][t] = jnp.where(inside, field[f][t] + TIME_STEP * steps[f], 0.0)
    for t in range(2, TH + 2):
        steps = rates(first, inverse[t], t)
        for f in range(FIELDS):
            second = 0.5 * (field[f][t] + first[f][t] + TIME_STEP * steps[f])
            for p in range(PAIRS):
                start = (t - 2) * TILE * ROWS + f * PAIRS + p
                out_ref[pl.ds(start, TILE, stride=ROWS), :] = second[p * TILE : (p + 1) * TILE]


def rotate_kernel(shift_ref, visc_ref, in_ref, out_ref, twice_ref):
    mine = lax.axis_index("phi") % TILE
    lane = lax.broadcasted_iota(jnp.int32, (PHI, LANES), 1)
    for p in range(PAIRS):
        radius = mine + p * TILE
        shift = shift_ref[radius]
        nu = visc_ref[radius]
        hops = lax.shift_right_logical(shift, 7)
        rest = jnp.bitwise_and(shift, LANES - 1)
        wrapped = lane < rest

        def shifted(f):
            turned = pltpu.roll(in_ref[pl.ds(f * PAIRS + p, PHI, stride=ROWS), :], rest, 1)
            slot = f * PAIRS + p
            twice_ref[slot, :PHI] = turned
            twice_ref[slot, PHI:] = turned
            near = twice_ref[slot, pl.ds(PHI - hops, PHI), :]
            far = twice_ref[slot, pl.ds(PHI - 1 - hops, PHI), :]
            return jnp.where(wrapped, far, near)

        def put(f, value):
            out_ref[pl.ds(f * PAIRS + p, PHI, stride=ROWS), :] = value

        def sides(value):
            right = pltpu.roll(value, 1, 1)
            left = pltpu.roll(value, LANES - 1, 1)
            behind = jnp.where(lane == 0, pltpu.roll(right, 1, 0), right)
            ahead = jnp.where(lane == LANES - 1, pltpu.roll(left, PHI - 1, 0), left)
            return behind, ahead

        rho = shifted(0)
        put(0, rho)
        for f in range(2, FIELDS):
            value = shifted(f)
            behind, ahead = sides(value)
            put(f, value + nu * (ahead - 2.0 * value + behind))
            if f == FIELDS - 1:
                slope = 0.5 * (ahead - behind)
                put(1, shifted(1) + nu * rho * slope * slope)


def unpack_kernel(in_ref, rho_ref, en_ref, vel_ref):
    for f in range(FIELDS):
        for t in range(TH):
            for p in range(PAIRS):
                start = t * TILE * ROWS + f * PAIRS + p
                value = in_ref[pl.ds(start, TILE, stride=ROWS), :]
                span = slice(p * TILE, (p + 1) * TILE)
                if f == 0:
                    rho_ref[t, span] = value
                elif f == 1:
                    en_ref[t, span] = value
                else:
                    vel_ref[f - 2, t, span] = value


def vmem():
    return pl.BlockSpec(memory_space=pltpu.VMEM)


def smem():
    return pl.BlockSpec(memory_space=pltpu.SMEM)


def near(value):
    return pltpu.with_memory_space_constraint(value, pltpu.VMEM)


def per_device(density, energy, velocity, shifts, viscosity):
    thetas = lax.axis_size("theta")
    row = lax.axis_index("row")
    swap = [(0, 1), (1, 0)]
    sibling = [near(lax.ppermute(value, "row", swap)) for value in (velocity, density, energy)]
    sibling = sibling[1:] + sibling[:1]
    fields, hops, nu = pl.pallas_call(
        pack_kernel,
        out_shape=(
            pltpu.VMEM((FIELDS,) + density.shape, jnp.float32),
            pltpu.SMEM(shifts.shape, jnp.int32),
            pltpu.SMEM(viscosity.shape, jnp.float32),
        ),
        in_specs=[pl.BlockSpec(memory_space=pl.ANY)] * 5,
        out_specs=(vmem(), smem(), smem()),
        scratch_shapes=[pltpu.SemaphoreType.DMA((5,))],
        name="pack",
    )(density, energy, velocity, shifts, viscosity)
    upward = [(i, (i + 1) % thetas) for i in range(thetas)]
    downward = [(j, i) for i, j in upward]
    message = pltpu.VMEM((BODY + TILE, LANES), jnp.float32)
    last, first = pl.pallas_call(
        build_kernel,
        out_shape=(message, message),
        in_specs=[vmem()] * 4,
        out_specs=(vmem(), vmem()),
        name="build",
    )(near(fields), *sibling)
    lo = lax.ppermute(last, "theta", upward)
    hi = lax.ppermute(first, "theta", downward)
    flat = pltpu.VMEM((PHI * ROWS, LANES), jnp.float32)
    second = pl.pallas_call(
        stencil_kernel,
        out_shape=flat,
        in_specs=[vmem()] * 6,
        out_specs=vmem(),
        name="stencil",
    )(near(fields), *sibling, near(lo), near(hi))

    def exchange(value):
        value = lax.all_to_all(value.reshape(-1), "phi", 0, 0, tiled=True)
        return value.reshape(PHI * ROWS, LANES)

    turned = pl.pallas_call(
        rotate_kernel,
        out_shape=flat,
        in_specs=[smem(), smem(), vmem()],
        out_specs=vmem(),
        scratch_shapes=[pltpu.VMEM((ROWS, 2 * PHI, LANES), jnp.float32)],
        name="rotate",
    )(
        pltpu.with_memory_space_constraint(hops, pltpu.SMEM),
        pltpu.with_memory_space_constraint(nu, pltpu.SMEM),
        near(exchange(second)),
    )
    block = jax.ShapeDtypeStruct(density.shape, jnp.float32)
    return pl.pallas_call(
        unpack_kernel,
        out_shape=(block, block, jax.ShapeDtypeStruct(velocity.shape, jnp.float32)),
        in_specs=[vmem()],
        out_specs=(vmem(), vmem(), vmem()),
        name="unpack",
    )(near(exchange(turned)))


def solution(mesh):
    return jax.shard_map(
        per_device,
        mesh=mesh,
        in_specs=(
            P("theta", "row", "phi"),
            P("theta", "row", "phi"),
            P(None, "theta", "row", "phi"),
            P("row"),
            P("row"),
        ),
        out_specs=(
            P("theta", "row", "phi"),
            P("theta", "row", "phi"),
            P(None, "theta", "row", "phi"),
        ),
        check_vma=False,
    )
```

```python
import jax
import jax.numpy as jnp
from jax import lax
from jax.experimental import pallas as pl
from jax.experimental.pallas import tpu as pltpu
from jax.sharding import PartitionSpec as P

GAMMA_LESS = 0.4
TIME_STEP = 0.4
DAMPING = 1.0
ROTATION = 0.5

FIELDS = 5
TH = 4
CR = 16
LANES = 128
TILE = 8
PHI = 32
PAIRS = TH * CR // PHI
ROWS = FIELDS * PAIRS
BODY = FIELDS * 2 * CR


def face(q_lo, q_hi, u_lo, u_hi):
    return 0.25 * (u_lo + u_hi) * (q_lo + q_hi) - 0.5 * DAMPING * (q_hi - q_lo)


def up(value):
    return pltpu.roll(value, value.shape[0] - 1, 0)


def down(value):
    return pltpu.roll(value, 1, 0)


def rates(field, inv_rho, t):
    rho, en, vr, vt, vp = (field[f] for f in range(FIELDS))
    vr_hi = up(vr[t])
    out = []

    def divergence(q, q_hi):
        flux = face(q[t], q_hi, vr[t], vr_hi)
        radial = flux - down(flux)
        polar = face(q[t], q[t + 1], vt[t], vt[t + 1]) - face(q[t - 1], q[t], vt[t - 1], vt[t])
        return radial + polar

    en_hi = up(en[t])
    d_rho = -divergence(rho, up(rho[t]))
    d_en = -divergence(en, en_hi)
    d_vp = -divergence(vp, up(vp[t])) - 0.5 * ROTATION * vr[t]
    grad_r = 0.5 * GAMMA_LESS * (en_hi - down(en[t]))
    grad_t = 0.5 * GAMMA_LESS * (en[t + 1] - en[t - 1])
    lap_r = vr[t + 1] + vr[t - 1] + vr_hi + down(vr[t]) - 4.0 * vr[t]
    lap_t = vt[t + 1] + vt[t - 1] + up(vt[t]) + down(vt[t]) - 4.0 * vt[t]
    d_vr = -grad_r * inv_rho + 0.5 * DAMPING * lap_r + 2.0 * ROTATION * vp[t]
    d_vt = -grad_t * inv_rho + 0.5 * DAMPING * lap_t
    return d_rho, d_en, d_vr, d_vt, d_vp


def pack_kernel(rho_ref, en_ref, vel_ref, shift_ref, visc_ref, out_ref, hop_ref, nu_ref, sems):
    copies = [
        pltpu.make_async_copy(shift_ref, hop_ref, sems.at[3]),
        pltpu.make_async_copy(visc_ref, nu_ref, sems.at[4]),
        pltpu.make_async_copy(rho_ref, out_ref.at[0], sems.at[0]),
        pltpu.make_async_copy(en_ref, out_ref.at[1], sems.at[1]),
        pltpu.make_async_copy(vel_ref, out_ref.at[2:], sems.at[2]),
    ]
    for copy in copies:
        copy.start()
    for copy in copies:
        copy.wait()


def side_of(refs, f, t):
    return refs[0].at[t] if f == 0 else refs[1].at[t] if f == 1 else refs[2].at[f - 2, t]


def build_kernel(own_ref, sib_rho, sib_en, sib_vel, up_ref, down_ref):
    border = (CR - 1) * lax.axis_index("row")
    sib = (sib_rho, sib_en, sib_vel)
    for out_ref, low, corner in ((up_ref, TH - 2, TH - 1), (down_ref, 0, 0)):
        out_ref[BODY:] = jnp.zeros((TILE, LANES), jnp.float32)
        for f in range(FIELDS):
            for t in range(2):
                out_ref[(2 * f + t) * CR : (2 * f + t + 1) * CR] = own_ref[f, low + t]
            out_ref[BODY + f : BODY + f + 1] = side_of(sib, f, corner)[pl.ds(border, 1), :]


class Block:
    def __init__(self, own_ref, sib, lo_ref=None, hi_ref=None):
        row = lax.axis_index("row")
        theta = lax.axis_index("theta")
        self.row, self.own_ref, self.sib, self.halo = row, own_ref, sib, (lo_ref, hi_ref)
        pos = lax.broadcasted_iota(jnp.int32, (TILE, LANES), 0)
        first_pos = (TILE - 2) * row
        self.at_first, self.at_second = pos == first_pos, pos == first_pos + 1
        at_border = pos == (TILE - 1) * row
        self.near = jnp.concatenate([jnp.ones((CR, LANES), jnp.bool_), at_border], 0)
        self.below = self.near & (theta > 0)
        self.above = self.near & (theta < lax.axis_size("theta") - 1)
        self.nothing = jnp.zeros((TILE, LANES), jnp.float32)

    def inside(self, t):
        return self.below if t < 2 else self.above if t >= TH + 2 else self.near

    def wide(self, f, t):
        if 2 <= t < TH + 2:
            side = side_of(self.sib, f, t - 2)
            one = spread(side[pl.ds((CR - 2) * self.row, 1), :])
            two = spread(side[pl.ds((CR - 2) * self.row + 1, 1), :])
            tile = jnp.where(self.at_first, one, jnp.where(self.at_second, two, self.nothing))
            return jnp.concatenate([self.own_ref[f, t - 2], tile], 0)
        ref = self.halo[t >= 2]
        start = (2 * f + t % 2) * CR
        tile = self.nothing
        if t in (1, TH + 2):
            tile = spread(ref[BODY + f : BODY + f + 1])
        whole = jnp.concatenate([ref[start : start + CR], tile], 0)
        return jnp.where(self.inside(t), whole, 0.0)

    def inverse(self, field, t):
        return 1.0 / jnp.where(self.inside(t), field[0][t], 1.0)

    def first(self, field, inverse, t):
        steps = rates(field, inverse, t)
        return [jnp.where(self.inside(t), field[f][t] + TIME_STEP * steps[f], 0.0) for f in range(FIELDS)]


def spread(line):
    return jnp.broadcast_to(line, (TILE, LANES))


def inner_kernel(own_ref, sib_rho, sib_en, sib_vel, first_ref, inv_ref):
    block = Block(own_ref, (sib_rho, sib_en, sib_vel))
    field = [[block.wide(f, t) if 2 <= t < TH + 2 else None for t in range(TH + 4)] for f in range(FIELDS)]
    for t in range(2, TH + 2):
        inverse = block.inverse(field, t)
        inv_ref[t - 2] = inverse
        if 2 < t < TH + 1:
            for f, value in enumerate(block.first(field, inverse, t)):
                first_ref[f, t - 3] = value


def stencil_kernel(own_ref, sib_rho, sib_en, sib_vel, lo_ref, hi_ref, first_ref, inv_ref, out_ref):
    block = Block(own_ref, (sib_rho, sib_en, sib_vel), lo_ref, hi_ref)
    field = [[block.wide(f, t) for t in range(TH + 4)] for f in range(FIELDS)]
    first = [[None] * (TH + 4) for _ in range(FIELDS)]
    for t in range(1, TH + 3):
        if 2 < t < TH + 1:
            values = [first_ref[f, t - 3] for f in range(FIELDS)]
        else:
            inverse = inv_ref[t - 2] if 2 <= t < TH + 2 else block.inverse(field, t)
            values = block.first(field, inverse, t)
        for f in range(FIELDS):
            first[f][t] = values[f]
    for t in range(2, TH + 2):
        steps = rates(first, inv_ref[t - 2], t)
        for f in range(FIELDS):
            second = 0.5 * (field[f][t] + first[f][t] + TIME_STEP * steps[f])
            for p in range(PAIRS):
                start = (t - 2) * TILE * ROWS + f * PAIRS + p
                out_ref[pl.ds(start, TILE, stride=ROWS), :] = second[p * TILE : (p + 1) * TILE]


def rotate_kernel(shift_ref, visc_ref, in_ref, out_ref, twice_ref):
    mine = lax.axis_index("phi") % TILE
    lane = lax.broadcasted_iota(jnp.int32, (PHI, LANES), 1)
    for p in range(PAIRS):
        radius = mine + p * TILE
        shift = shift_ref[radius]
        nu = visc_ref[radius]
        hops = lax.shift_right_logical(shift, 7)
        rest = jnp.bitwise_and(shift, LANES - 1)
        wrapped = lane < rest

        def shifted(f):
            turned = pltpu.roll(in_ref[pl.ds(f * PAIRS + p, PHI, stride=ROWS), :], rest, 1)
            slot = f * PAIRS + p
            twice_ref[slot, :PHI] = turned
            twice_ref[slot, PHI:] = turned
            near = twice_ref[slot, pl.ds(PHI - hops, PHI), :]
            far = twice_ref[slot, pl.ds(PHI - 1 - hops, PHI), :]
            return jnp.where(wrapped, far, near)

        def put(f, value):
            out_ref[pl.ds(f * PAIRS + p, PHI, stride=ROWS), :] = value

        def sides(value):
            right = pltpu.roll(value, 1, 1)
            left = pltpu.roll(value, LANES - 1, 1)
            behind = jnp.where(lane == 0, pltpu.roll(right, 1, 0), right)
            ahead = jnp.where(lane == LANES - 1, pltpu.roll(left, PHI - 1, 0), left)
            return behind, ahead

        rho = shifted(0)
        put(0, rho)
        for f in range(2, FIELDS):
            value = shifted(f)
            behind, ahead = sides(value)
            put(f, value + nu * (ahead - 2.0 * value + behind))
            if f == FIELDS - 1:
                slope = 0.5 * (ahead - behind)
                put(1, shifted(1) + nu * rho * slope * slope)


def unpack_kernel(in_ref, rho_ref, en_ref, vel_ref):
    for f in range(FIELDS):
        for t in range(TH):
            for p in range(PAIRS):
                start = t * TILE * ROWS + f * PAIRS + p
                value = in_ref[pl.ds(start, TILE, stride=ROWS), :]
                span = slice(p * TILE, (p + 1) * TILE)
                if f == 0:
                    rho_ref[t, span] = value
                elif f == 1:
                    en_ref[t, span] = value
                else:
                    vel_ref[f - 2, t, span] = value


def vmem():
    return pl.BlockSpec(memory_space=pltpu.VMEM)


def smem():
    return pl.BlockSpec(memory_space=pltpu.SMEM)


def near(value):
    return pltpu.with_memory_space_constraint(value, pltpu.VMEM)


def per_device(density, energy, velocity, shifts, viscosity):
    thetas = lax.axis_size("theta")
    row = lax.axis_index("row")
    swap = [(0, 1), (1, 0)]
    sibling = [near(lax.ppermute(value, "row", swap)) for value in (velocity, density, energy)]
    sibling = sibling[1:] + sibling[:1]
    fields, hops, nu = pl.pallas_call(
        pack_kernel,
        out_shape=(
            pltpu.VMEM((FIELDS,) + density.shape, jnp.float32),
            pltpu.SMEM(shifts.shape, jnp.int32),
            pltpu.SMEM(viscosity.shape, jnp.float32),
        ),
        in_specs=[pl.BlockSpec(memory_space=pl.ANY)] * 5,
        out_specs=(vmem(), smem(), smem()),
        scratch_shapes=[pltpu.SemaphoreType.DMA((5,))],
        name="pack",
    )(density, energy, velocity, shifts, viscosity)
    upward = [(i, (i + 1) % thetas) for i in range(thetas)]
    downward = [(j, i) for i, j in upward]
    message = pltpu.VMEM((BODY + TILE, LANES), jnp.float32)
    last, first = pl.pallas_call(
        build_kernel,
        out_shape=(message, message),
        in_specs=[vmem()] * 4,
        out_specs=(vmem(), vmem()),
        name="build",
    )(near(fields), *sibling)
    lo = lax.ppermute(last, "theta", upward)
    hi = lax.ppermute(first, "theta", downward)
    tall = CR + TILE
    first_one, inverse = pl.pallas_call(
        inner_kernel,
        out_shape=(
            pltpu.VMEM((FIELDS, TH - 2, tall, LANES), jnp.float32),
            pltpu.VMEM((TH, tall, LANES), jnp.float32),
        ),
        in_specs=[vmem()] * 4,
        out_specs=(vmem(), vmem()),
        name="inner",
    )(near(fields), *sibling)
    flat = pltpu.VMEM((PHI * ROWS, LANES), jnp.float32)
    second = pl.pallas_call(
        stencil_kernel,
        out_shape=flat,
        in_specs=[vmem()] * 8,
        out_specs=vmem(),
        name="stencil",
    )(near(fields), *sibling, near(lo), near(hi), near(first_one), near(inverse))

    def exchange(value):
        value = lax.all_to_all(value.reshape(-1), "phi", 0, 0, tiled=True)
        return value.reshape(PHI * ROWS, LANES)

    turned = pl.pallas_call(
        rotate_kernel,
        out_shape=flat,
        in_specs=[smem(), smem(), vmem()],
        out_specs=vmem(),
        scratch_shapes=[pltpu.VMEM((ROWS, 2 * PHI, LANES), jnp.float32)],
        name="rotate",
    )(
        pltpu.with_memory_space_constraint(hops, pltpu.SMEM),
        pltpu.with_memory_space_constraint(nu, pltpu.SMEM),
        near(exchange(second)),
    )
    block = jax.ShapeDtypeStruct(density.shape, jnp.float32)
    return pl.pallas_call(
        unpack_kernel,
        out_shape=(block, block, jax.ShapeDtypeStruct(velocity.shape, jnp.float32)),
        in_specs=[vmem()],
        out_specs=(vmem(), vmem(), vmem()),
        name="unpack",
    )(near(exchange(turned)))


def solution(mesh):
    return jax.shard_map(
        per_device,
        mesh=mesh,
        in_specs=(
            P("theta", "row", "phi"),
            P("theta", "row", "phi"),
            P(None, "theta", "row", "phi"),
            P("row"),
            P("row"),
        ),
        out_specs=(
            P("theta", "row", "phi"),
            P("theta", "row", "phi"),
            P(None, "theta", "row", "phi"),
        ),
        check_vma=False,
    )
```

```python
import jax
import jax.numpy as jnp
from jax import lax
from jax.experimental import pallas as pl
from jax.experimental.pallas import tpu as pltpu
from jax.sharding import PartitionSpec as P

GAMMA_LESS = 0.4
TIME_STEP = 0.4
DAMPING = 1.0
ROTATION = 0.5

FIELDS = 5
TH = 4
CR = 16
LANES = 128
TILE = 8
PHI = 32
PAIRS = TH * CR // PHI
ROWS = FIELDS * PAIRS
BODY = FIELDS * 2 * CR


def face(q_lo, q_hi, u_lo, u_hi):
    return 0.25 * (u_lo + u_hi) * (q_lo + q_hi) - 0.5 * DAMPING * (q_hi - q_lo)


def up(value):
    return pltpu.roll(value, value.shape[0] - 1, 0)


def down(value):
    return pltpu.roll(value, 1, 0)


def rates(field, inv_rho, t):
    rho, en, vr, vt, vp = (field[f] for f in range(FIELDS))
    vr_hi = up(vr[t])
    out = []

    def divergence(q, q_hi):
        flux = face(q[t], q_hi, vr[t], vr_hi)
        radial = flux - down(flux)
        polar = face(q[t], q[t + 1], vt[t], vt[t + 1]) - face(q[t - 1], q[t], vt[t - 1], vt[t])
        return radial + polar

    en_hi = up(en[t])
    d_rho = -divergence(rho, up(rho[t]))
    d_en = -divergence(en, en_hi)
    d_vp = -divergence(vp, up(vp[t])) - 0.5 * ROTATION * vr[t]
    grad_r = 0.5 * GAMMA_LESS * (en_hi - down(en[t]))
    grad_t = 0.5 * GAMMA_LESS * (en[t + 1] - en[t - 1])
    lap_r = vr[t + 1] + vr[t - 1] + vr_hi + down(vr[t]) - 4.0 * vr[t]
    lap_t = vt[t + 1] + vt[t - 1] + up(vt[t]) + down(vt[t]) - 4.0 * vt[t]
    d_vr = -grad_r * inv_rho + 0.5 * DAMPING * lap_r + 2.0 * ROTATION * vp[t]
    d_vt = -grad_t * inv_rho + 0.5 * DAMPING * lap_t
    return d_rho, d_en, d_vr, d_vt, d_vp


def pack_kernel(rho_ref, en_ref, vel_ref, shift_ref, visc_ref, out_ref, hop_ref, nu_ref, sems):
    copies = [
        pltpu.make_async_copy(shift_ref, hop_ref, sems.at[3]),
        pltpu.make_async_copy(visc_ref, nu_ref, sems.at[4]),
        pltpu.make_async_copy(rho_ref, out_ref.at[0], sems.at[0]),
        pltpu.make_async_copy(en_ref, out_ref.at[1], sems.at[1]),
        pltpu.make_async_copy(vel_ref, out_ref.at[2:], sems.at[2]),
    ]
    for copy in copies:
        copy.start()
    for copy in copies:
        copy.wait()


def side_of(refs, f, t):
    return refs[0].at[t] if f == 0 else refs[1].at[t] if f == 1 else refs[2].at[f - 2, t]


def build_kernel(own_ref, sib_rho, sib_en, sib_vel, up_ref, down_ref):
    border = (CR - 1) * lax.axis_index("row")
    sib = (sib_rho, sib_en, sib_vel)
    for out_ref, low, corner in ((up_ref, TH - 2, TH - 1), (down_ref, 0, 0)):
        out_ref[BODY:] = jnp.zeros((TILE, LANES), jnp.float32)
        for f in range(FIELDS):
            for t in range(2):
                out_ref[(2 * f + t) * CR : (2 * f + t + 1) * CR] = own_ref[f, low + t]
            out_ref[BODY + f : BODY + f + 1] = side_of(sib, f, corner)[pl.ds(border, 1), :]


class Block:
    def __init__(self, own_ref, sib, lo_ref=None, hi_ref=None):
        row = lax.axis_index("row")
        theta = lax.axis_index("theta")
        self.row, self.own_ref, self.sib, self.halo = row, own_ref, sib, (lo_ref, hi_ref)
        pos = lax.broadcasted_iota(jnp.int32, (TILE, LANES), 0)
        first_pos = (TILE - 2) * row
        self.at_first, self.at_second = pos == first_pos, pos == first_pos + 1
        at_border = pos == (TILE - 1) * row
        self.near = jnp.concatenate([jnp.ones((CR, LANES), jnp.bool_), at_border], 0)
        self.below = self.near & (theta > 0)
        self.above = self.near & (theta < lax.axis_size("theta") - 1)
        self.nothing = jnp.zeros((TILE, LANES), jnp.float32)

    def inside(self, t):
        return self.below if t < 2 else self.above if t >= TH + 2 else self.near

    def wide(self, f, t):
        if 2 <= t < TH + 2:
            side = side_of(self.sib, f, t - 2)
            one = spread(side[pl.ds((CR - 2) * self.row, 1), :])
            two = spread(side[pl.ds((CR - 2) * self.row + 1, 1), :])
            tile = jnp.where(self.at_first, one, jnp.where(self.at_second, two, self.nothing))
            return jnp.concatenate([self.own_ref[f, t - 2], tile], 0)
        ref = self.halo[t >= 2]
        start = (2 * f + t % 2) * CR
        tile = self.nothing
        if t in (1, TH + 2):
            tile = spread(ref[BODY + f : BODY + f + 1])
        whole = jnp.concatenate([ref[start : start + CR], tile], 0)
        return jnp.where(self.inside(t), whole, 0.0)

    def inverse(self, field, t):
        return 1.0 / jnp.where(self.inside(t), field[0][t], 1.0)

    def first(self, field, inverse, t):
        steps = rates(field, inverse, t)
        return [jnp.where(self.inside(t), field[f][t] + TIME_STEP * steps[f], 0.0) for f in range(FIELDS)]


def spread(line):
    return jnp.broadcast_to(line, (TILE, LANES))


def inner_kernel(own_ref, sib_rho, sib_en, sib_vel, first_ref, inv_ref):
    block = Block(own_ref, (sib_rho, sib_en, sib_vel))
    field = [[block.wide(f, t) if 2 <= t < TH + 2 else None for t in range(TH + 4)] for f in range(FIELDS)]
    for t in range(2, TH + 2):
        inverse = block.inverse(field, t)
        inv_ref[t - 2] = inverse
        if 2 < t < TH + 1:
            for f, value in enumerate(block.first(field, inverse, t)):
                first_ref[f, t - 3] = value


def stencil_kernel(own_ref, sib_rho, sib_en, sib_vel, lo_ref, hi_ref, first_ref, inv_ref, out_ref):
    block = Block(own_ref, (sib_rho, sib_en, sib_vel), lo_ref, hi_ref)
    field = [[block.wide(f, t) for t in range(TH + 4)] for f in range(FIELDS)]
    first = [[None] * (TH + 4) for _ in range(FIELDS)]
    for t in range(1, TH + 3):
        if 2 < t < TH + 1:
            values = [first_ref[f, t - 3] for f in range(FIELDS)]
        else:
            inverse = inv_ref[t - 2] if 2 <= t < TH + 2 else block.inverse(field, t)
            values = block.first(field, inverse, t)
        for f in range(FIELDS):
            first[f][t] = values[f]
    for t in range(2, TH + 2):
        steps = rates(first, inv_ref[t - 2], t)
        for f in range(FIELDS):
            second = 0.5 * (field[f][t] + first[f][t] + TIME_STEP * steps[f])
            for p in range(PAIRS):
                start = (t - 2) * TILE * ROWS + f * PAIRS + p
                out_ref[pl.ds(start, TILE, stride=ROWS), :] = second[p * TILE : (p + 1) * TILE]


def rotate_kernel(shift_ref, visc_ref, in_ref, out_ref):
    mine = lax.axis_index("phi") % TILE
    lane = lax.broadcasted_iota(jnp.int32, (PHI, LANES), 1)
    for p in range(PAIRS):
        radius = mine + p * TILE
        shift = shift_ref[radius]
        nu = visc_ref[radius]
        hops = lax.shift_right_logical(shift, 7)
        rest = jnp.bitwise_and(shift, LANES - 1)
        wrapped = lane < rest

        def shifted(f):
            turned = pltpu.roll(in_ref[pl.ds(f * PAIRS + p, PHI, stride=ROWS), :], rest, 1)
            near = pltpu.roll(turned, hops, 0)
            return jnp.where(wrapped, pltpu.roll(near, 1, 0), near)

        def put(f, value):
            out_ref[pl.ds(f * PAIRS + p, PHI, stride=ROWS), :] = value

        def sides(value):
            right = pltpu.roll(value, 1, 1)
            left = pltpu.roll(value, LANES - 1, 1)
            behind = jnp.where(lane == 0, pltpu.roll(right, 1, 0), right)
            ahead = jnp.where(lane == LANES - 1, pltpu.roll(left, PHI - 1, 0), left)
            return behind, ahead

        rho = shifted(0)
        put(0, rho)
        for f in range(2, FIELDS):
            value = shifted(f)
            behind, ahead = sides(value)
            put(f, value + nu * (ahead - 2.0 * value + behind))
            if f == FIELDS - 1:
                slope = 0.5 * (ahead - behind)
                put(1, shifted(1) + nu * rho * slope * slope)


def unpack_kernel(in_ref, rho_ref, en_ref, vel_ref):
    for f in range(FIELDS):
        for t in range(TH):
            for p in range(PAIRS):
                start = t * TILE * ROWS + f * PAIRS + p
                value = in_ref[pl.ds(start, TILE, stride=ROWS), :]
                span = slice(p * TILE, (p + 1) * TILE)
                if f == 0:
                    rho_ref[t, span] = value
                elif f == 1:
                    en_ref[t, span] = value
                else:
                    vel_ref[f - 2, t, span] = value


def vmem():
    return pl.BlockSpec(memory_space=pltpu.VMEM)


def smem():
    return pl.BlockSpec(memory_space=pltpu.SMEM)


def near(value):
    return pltpu.with_memory_space_constraint(value, pltpu.VMEM)


def per_device(density, energy, velocity, shifts, viscosity):
    thetas = lax.axis_size("theta")
    row = lax.axis_index("row")
    swap = [(0, 1), (1, 0)]
    sibling = [near(lax.ppermute(value, "row", swap)) for value in (velocity, density, energy)]
    sibling = sibling[1:] + sibling[:1]
    fields, hops, nu = pl.pallas_call(
        pack_kernel,
        out_shape=(
            pltpu.VMEM((FIELDS,) + density.shape, jnp.float32),
            pltpu.SMEM(shifts.shape, jnp.int32),
            pltpu.SMEM(viscosity.shape, jnp.float32),
        ),
        in_specs=[pl.BlockSpec(memory_space=pl.ANY)] * 5,
        out_specs=(vmem(), smem(), smem()),
        scratch_shapes=[pltpu.SemaphoreType.DMA((5,))],
        name="pack",
    )(density, energy, velocity, shifts, viscosity)
    upward = [(i, (i + 1) % thetas) for i in range(thetas)]
    downward = [(j, i) for i, j in upward]
    message = pltpu.VMEM((BODY + TILE, LANES), jnp.float32)
    last, first = pl.pallas_call(
        build_kernel,
        out_shape=(message, message),
        in_specs=[vmem()] * 4,
        out_specs=(vmem(), vmem()),
        name="build",
    )(near(fields), *sibling)
    lo = lax.ppermute(last, "theta", upward)
    hi = lax.ppermute(first, "theta", downward)
    tall = CR + TILE
    first_one, inverse = pl.pallas_call(
        inner_kernel,
        out_shape=(
            pltpu.VMEM((FIELDS, TH - 2, tall, LANES), jnp.float32),
            pltpu.VMEM((TH, tall, LANES), jnp.float32),
        ),
        in_specs=[vmem()] * 4,
        out_specs=(vmem(), vmem()),
        name="inner",
    )(near(fields), *sibling)
    flat = pltpu.VMEM((PHI * ROWS, LANES), jnp.float32)
    second = pl.pallas_call(
        stencil_kernel,
        out_shape=flat,
        in_specs=[vmem()] * 8,
        out_specs=vmem(),
        name="stencil",
    )(near(fields), *sibling, near(lo), near(hi), near(first_one), near(inverse))

    def exchange(value):
        value = lax.all_to_all(value.reshape(-1), "phi", 0, 0, tiled=True)
        return value.reshape(PHI * ROWS, LANES)

    turned = pl.pallas_call(
        rotate_kernel,
        out_shape=flat,
        in_specs=[smem(), smem(), vmem()],
        out_specs=vmem(),
        name="rotate",
    )(
        pltpu.with_memory_space_constraint(hops, pltpu.SMEM),
        pltpu.with_memory_space_constraint(nu, pltpu.SMEM),
        near(exchange(second)),
    )
    block = jax.ShapeDtypeStruct(density.shape, jnp.float32)
    return pl.pallas_call(
        unpack_kernel,
        out_shape=(block, block, jax.ShapeDtypeStruct(velocity.shape, jnp.float32)),
        in_specs=[vmem()],
        out_specs=(vmem(), vmem(), vmem()),
        name="unpack",
    )(near(exchange(turned)))


def solution(mesh):
    return jax.shard_map(
        per_device,
        mesh=mesh,
        in_specs=(
            P("theta", "row", "phi"),
            P("theta", "row", "phi"),
            P(None, "theta", "row", "phi"),
            P("row"),
            P("row"),
        ),
        out_specs=(
            P("theta", "row", "phi"),
            P("theta", "row", "phi"),
            P(None, "theta", "row", "phi"),
        ),
        check_vma=False,
    )
```

```python
import jax
import jax.numpy as jnp
from jax import lax
from jax.experimental import pallas as pl
from jax.experimental.pallas import tpu as pltpu
from jax.sharding import PartitionSpec as P

GAMMA_LESS = 0.4
TIME_STEP = 0.4
DAMPING = 1.0
ROTATION = 0.5

FIELDS = 5
TH = 4
CR = 16
LANES = 128
TILE = 8
PHI = 32
PAIRS = TH * CR // PHI
ROWS = FIELDS * PAIRS
BODY = FIELDS * 2 * CR


def face(q_lo, q_hi, u_lo, u_hi):
    return 0.25 * (u_lo + u_hi) * (q_lo + q_hi) - 0.5 * DAMPING * (q_hi - q_lo)


def up(value):
    return pltpu.roll(value, value.shape[0] - 1, 0)


def down(value):
    return pltpu.roll(value, 1, 0)


def rates(field, inv_rho, t, skip=0):
    rho, en, vr, vt, vp = (field[f] for f in range(FIELDS))
    vr_hi = up(vr[t])

    def at(q, step):
        return 0.0 if step == skip else q[t + step]

    def divergence(q, q_hi):
        flux = face(q[t], q_hi, vr[t], vr_hi)
        total = flux - down(flux)
        if skip != 1:
            total = total + face(q[t], q[t + 1], vt[t], vt[t + 1])
        if skip != -1:
            total = total - face(q[t - 1], q[t], vt[t - 1], vt[t])
        return total

    en_hi = up(en[t])
    d_rho = -divergence(rho, up(rho[t]))
    d_en = -divergence(en, en_hi)
    d_vp = -divergence(vp, up(vp[t])) - 0.5 * ROTATION * vr[t]
    grad_r = 0.5 * GAMMA_LESS * (en_hi - down(en[t]))
    grad_t = 0.5 * GAMMA_LESS * (at(en, 1) - at(en, -1))
    lap_r = at(vr, 1) + at(vr, -1) + vr_hi + down(vr[t]) - 4.0 * vr[t]
    lap_t = at(vt, 1) + at(vt, -1) + up(vt[t]) + down(vt[t]) - 4.0 * vt[t]
    d_vr = -grad_r * inv_rho + 0.5 * DAMPING * lap_r + 2.0 * ROTATION * vp[t]
    d_vt = -grad_t * inv_rho + 0.5 * DAMPING * lap_t
    return d_rho, d_en, d_vr, d_vt, d_vp


def neighbour_rates(field, inv_rho, t, step):
    _, en, vr, vt, _ = (field[f] for f in range(FIELDS))
    lo, hi = min(t, t + step), max(t, t + step)

    def flux(q):
        return -step * face(q[lo], q[hi], vt[lo], vt[hi])

    d_vt = 0.5 * DAMPING * vt[t + step] - step * 0.5 * GAMMA_LESS * en[t + step] * inv_rho
    return flux(field[0]), flux(en), 0.5 * DAMPING * vr[t + step], d_vt, flux(field[4])


def pack_kernel(rho_ref, en_ref, vel_ref, shift_ref, visc_ref, out_ref, hop_ref, nu_ref, sems):
    copies = [
        pltpu.make_async_copy(shift_ref, hop_ref, sems.at[3]),
        pltpu.make_async_copy(visc_ref, nu_ref, sems.at[4]),
        pltpu.make_async_copy(rho_ref, out_ref.at[0], sems.at[0]),
        pltpu.make_async_copy(en_ref, out_ref.at[1], sems.at[1]),
        pltpu.make_async_copy(vel_ref, out_ref.at[2:], sems.at[2]),
    ]
    for copy in copies:
        copy.start()
    for copy in copies:
        copy.wait()


def side_of(refs, f, t):
    return refs[0].at[t] if f == 0 else refs[1].at[t] if f == 1 else refs[2].at[f - 2, t]


def build_kernel(own_ref, sib_rho, sib_en, sib_vel, up_ref, down_ref):
    border = (CR - 1) * lax.axis_index("row")
    sib = (sib_rho, sib_en, sib_vel)
    for out_ref, low, corner in ((up_ref, TH - 2, TH - 1), (down_ref, 0, 0)):
        out_ref[BODY:] = jnp.zeros((TILE, LANES), jnp.float32)
        for f in range(FIELDS):
            for t in range(2):
                out_ref[(2 * f + t) * CR : (2 * f + t + 1) * CR] = own_ref[f, low + t]
            out_ref[BODY + f : BODY + f + 1] = side_of(sib, f, corner)[pl.ds(border, 1), :]


class Block:
    def __init__(self, own_ref=None, sib=None, lo_ref=None, hi_ref=None):
        row = lax.axis_index("row")
        theta = lax.axis_index("theta")
        self.row, self.own_ref, self.sib, self.halo = row, own_ref, sib, (lo_ref, hi_ref)
        pos = lax.broadcasted_iota(jnp.int32, (TILE, LANES), 0)
        first_pos = (TILE - 2) * row
        self.at_first, self.at_second = pos == first_pos, pos == first_pos + 1
        at_border = pos == (TILE - 1) * row
        self.near = jnp.concatenate([jnp.ones((CR, LANES), jnp.bool_), at_border], 0)
        self.below = self.near & (theta > 0)
        self.above = self.near & (theta < lax.axis_size("theta") - 1)
        self.nothing = jnp.zeros((TILE, LANES), jnp.float32)

    def inside(self, t):
        return self.below if t < 2 else self.above if t >= TH + 2 else self.near

    def wide(self, f, t):
        if 2 <= t < TH + 2:
            side = side_of(self.sib, f, t - 2)
            one = spread(side[pl.ds((CR - 2) * self.row, 1), :])
            two = spread(side[pl.ds((CR - 2) * self.row + 1, 1), :])
            tile = jnp.where(self.at_first, one, jnp.where(self.at_second, two, self.nothing))
            return jnp.concatenate([self.own_ref[f, t - 2], tile], 0)
        ref = self.halo[t >= 2]
        start = (2 * f + t % 2) * CR
        tile = self.nothing
        if t in (1, TH + 2):
            tile = spread(ref[BODY + f : BODY + f + 1])
        whole = jnp.concatenate([ref[start : start + CR], tile], 0)
        return jnp.where(self.inside(t), whole, 0.0)

    def inverse(self, field, t):
        return 1.0 / jnp.where(self.inside(t), field[0][t], 1.0)

    def first(self, field, inverse, t, skip=0):
        steps = rates(field, inverse, t, skip)
        return [jnp.where(self.inside(t), field[f][t] + TIME_STEP * steps[f], 0.0) for f in range(FIELDS)]


def spread(line):
    return jnp.broadcast_to(line, (TILE, LANES))


def inner_kernel(own_ref, sib_rho, sib_en, sib_vel, wide_ref, first_ref, inv_ref):
    block = Block(own_ref, (sib_rho, sib_en, sib_vel))
    field = [[block.wide(f, t) if 2 <= t < TH + 2 else None for t in range(TH + 4)] for f in range(FIELDS)]
    for t in range(2, TH + 2):
        inverse = block.inverse(field, t)
        inv_ref[t - 2] = inverse
        for f in range(FIELDS):
            wide_ref[f, t - 2] = field[f][t]
        skip = -1 if t == 2 else 1 if t == TH + 1 else 0
        for f, value in enumerate(block.first(field, inverse, t, skip)):
            first_ref[f, t - 2] = value


def stencil_kernel(lo_ref, hi_ref, wide_ref, first_ref, inv_ref, out_ref):
    block = Block(lo_ref=lo_ref, hi_ref=hi_ref)
    field = [
        [wide_ref[f, t - 2] if 2 <= t < TH + 2 else block.wide(f, t) for t in range(TH + 4)]
        for f in range(FIELDS)
    ]
    first = [[None] * (TH + 4) for _ in range(FIELDS)]
    for t in range(1, TH + 3):
        if 2 <= t < TH + 2:
            values = [first_ref[f, t - 2] for f in range(FIELDS)]
            step = -1 if t == 2 else 1 if t == TH + 1 else 0
            if step:
                more = neighbour_rates(field, inv_ref[t - 2], t, step)
                values = [jnp.where(block.near, v + TIME_STEP * m, 0.0) for v, m in zip(values, more)]
        else:
            values = block.first(field, block.inverse(field, t), t)
        for f in range(FIELDS):
            first[f][t] = values[f]
    for t in range(2, TH + 2):
        steps = rates(first, inv_ref[t - 2], t)
        for f in range(FIELDS):
            second = 0.5 * (field[f][t] + first[f][t] + TIME_STEP * steps[f])
            for p in range(PAIRS):
                start = (t - 2) * TILE * ROWS + f * PAIRS + p
                out_ref[pl.ds(start, TILE, stride=ROWS), :] = second[p * TILE : (p + 1) * TILE]


def rotate_kernel(shift_ref, visc_ref, in_ref, out_ref):
    mine = lax.axis_index("phi") % TILE
    lane = lax.broadcasted_iota(jnp.int32, (PHI, LANES), 1)
    for p in range(PAIRS):
        radius = mine + p * TILE
        shift = shift_ref[radius]
        nu = visc_ref[radius]
        hops = lax.shift_right_logical(shift, 7)
        rest = jnp.bitwise_and(shift, LANES - 1)
        wrapped = lane < rest

        def shifted(f):
            turned = pltpu.roll(in_ref[pl.ds(f * PAIRS + p, PHI, stride=ROWS), :], rest, 1)
            near = pltpu.roll(turned, hops, 0)
            return jnp.where(wrapped, pltpu.roll(near, 1, 0), near)

        def put(f, value):
            out_ref[pl.ds(f * PAIRS + p, PHI, stride=ROWS), :] = value

        def sides(value):
            right = pltpu.roll(value, 1, 1)
            left = pltpu.roll(value, LANES - 1, 1)
            behind = jnp.where(lane == 0, pltpu.roll(right, 1, 0), right)
            ahead = jnp.where(lane == LANES - 1, pltpu.roll(left, PHI - 1, 0), left)
            return behind, ahead

        rho = shifted(0)
        put(0, rho)
        for f in range(2, FIELDS):
            value = shifted(f)
            behind, ahead = sides(value)
            put(f, value + nu * (ahead - 2.0 * value + behind))
            if f == FIELDS - 1:
                slope = 0.5 * (ahead - behind)
                put(1, shifted(1) + nu * rho * slope * slope)


def unpack_kernel(in_ref, rho_ref, en_ref, vel_ref):
    for f in range(FIELDS):
        for t in range(TH):
            for p in range(PAIRS):
                start = t * TILE * ROWS + f * PAIRS + p
                value = in_ref[pl.ds(start, TILE, stride=ROWS), :]
                span = slice(p * TILE, (p + 1) * TILE)
                if f == 0:
                    rho_ref[t, span] = value
                elif f == 1:
                    en_ref[t, span] = value
                else:
                    vel_ref[f - 2, t, span] = value


def vmem():
    return pl.BlockSpec(memory_space=pltpu.VMEM)


def smem():
    return pl.BlockSpec(memory_space=pltpu.SMEM)


def near(value):
    return pltpu.with_memory_space_constraint(value, pltpu.VMEM)


def per_device(density, energy, velocity, shifts, viscosity):
    thetas = lax.axis_size("theta")
    row = lax.axis_index("row")
    swap = [(0, 1), (1, 0)]
    sibling = [near(lax.ppermute(value, "row", swap)) for value in (velocity, density, energy)]
    sibling = sibling[1:] + sibling[:1]
    fields, hops, nu = pl.pallas_call(
        pack_kernel,
        out_shape=(
            pltpu.VMEM((FIELDS,) + density.shape, jnp.float32),
            pltpu.SMEM(shifts.shape, jnp.int32),
            pltpu.SMEM(viscosity.shape, jnp.float32),
        ),
        in_specs=[pl.BlockSpec(memory_space=pl.ANY)] * 5,
        out_specs=(vmem(), smem(), smem()),
        scratch_shapes=[pltpu.SemaphoreType.DMA((5,))],
        name="pack",
    )(density, energy, velocity, shifts, viscosity)
    upward = [(i, (i + 1) % thetas) for i in range(thetas)]
    downward = [(j, i) for i, j in upward]
    message = pltpu.VMEM((BODY + TILE, LANES), jnp.float32)
    last, first = pl.pallas_call(
        build_kernel,
        out_shape=(message, message),
        in_specs=[vmem()] * 4,
        out_specs=(vmem(), vmem()),
        name="build",
    )(near(fields), *sibling)
    lo = lax.ppermute(last, "theta", upward)
    hi = lax.ppermute(first, "theta", downward)
    tall = CR + TILE
    wide, first_one, inverse = pl.pallas_call(
        inner_kernel,
        out_shape=(
            pltpu.VMEM((FIELDS, TH, tall, LANES), jnp.float32),
            pltpu.VMEM((FIELDS, TH, tall, LANES), jnp.float32),
            pltpu.VMEM((TH, tall, LANES), jnp.float32),
        ),
        in_specs=[vmem()] * 4,
        out_specs=(vmem(), vmem(), vmem()),
        name="inner",
    )(near(fields), *sibling)
    flat = pltpu.VMEM((PHI * ROWS, LANES), jnp.float32)
    second = pl.pallas_call(
        stencil_kernel,
        out_shape=flat,
        in_specs=[vmem()] * 5,
        out_specs=vmem(),
        name="stencil",
    )(near(lo), near(hi), near(wide), near(first_one), near(inverse))

    def exchange(value):
        value = lax.all_to_all(value.reshape(-1), "phi", 0, 0, tiled=True)
        return value.reshape(PHI * ROWS, LANES)

    turned = pl.pallas_call(
        rotate_kernel,
        out_shape=flat,
        in_specs=[smem(), smem(), vmem()],
        out_specs=vmem(),
        name="rotate",
    )(
        pltpu.with_memory_space_constraint(hops, pltpu.SMEM),
        pltpu.with_memory_space_constraint(nu, pltpu.SMEM),
        near(exchange(second)),
    )
    block = jax.ShapeDtypeStruct(density.shape, jnp.float32)
    return pl.pallas_call(
        unpack_kernel,
        out_shape=(block, block, jax.ShapeDtypeStruct(velocity.shape, jnp.float32)),
        in_specs=[vmem()],
        out_specs=(vmem(), vmem(), vmem()),
        name="unpack",
    )(near(exchange(turned)))


def solution(mesh):
    return jax.shard_map(
        per_device,
        mesh=mesh,
        in_specs=(
            P("theta", "row", "phi"),
            P("theta", "row", "phi"),
            P(None, "theta", "row", "phi"),
            P("row"),
            P("row"),
        ),
        out_specs=(
            P("theta", "row", "phi"),
            P("theta", "row", "phi"),
            P(None, "theta", "row", "phi"),
        ),
        check_vma=False,
    )
```
